32 devices in a mesh: groups: 2 (over y), member: 2 (over core), fsdp: 8 (over z, x).
Axes of the slice: x: 2, y: 2, z: 4, core: 2. Of those that a mesh axis runs over, the one named last changes fastest.
Arguments:
- features: bfloat16 [16, 128, 4096], P(('groups', 'fsdp')), parts along dimension 0, may hold values from -6 to 6
- blocks: int32 [4, 2], P(('groups', 'member')), parts along dimension 0, may hold values from 0 to 7
- pair_labels: int32 [4, 4, 2], P(('groups', 'member')), parts along dimension 0, may hold values from 0 to 1, as said below
- ffn_gain: float32 [2, 4096], P('member'), may hold values from 0.5 to 2
- final_gain: float32 [2, 4096], P('member'), may hold values from 0.5 to 2
- score_head: float32 [2, 4096], P('member'), may hold values from -0.75 to 0.75
- w_gate: bfloat16 [2, 4096, 14336], P('member', None, 'fsdp'), may hold values from -0.09375 to 0.09375
- w_up: bfloat16 [2, 4096, 14336], P('member', None, 'fsdp'), may hold values from -1 to 1
- w_down: bfloat16 [2, 14336, 4096], P('member', 'fsdp'), may hold values from -1 to 1
Outputs:
- pair_loss: float32 [4], P(('groups', 'member')), parts along dimension 0
- grad_gate: bfloat16 [4, 4096, 14336], P(('groups', 'member'), None, 'fsdp'), parts along dimension 0
- grad_up: bfloat16 [4, 4096, 14336], P(('groups', 'member'), None, 'fsdp'), parts along dimension 0
- grad_down: bfloat16 [4, 14336, 4096], P(('groups', 'member'), 'fsdp'), parts along dimension 0
- grad_head: float32 [4, 4096], P(('groups', 'member'), 'fsdp'), parts along dimension 0
- grad_final_gain: float32 [4, 4096], P(('groups', 'member'), 'fsdp'), parts along dimension 0
- grad_ffn_gain: float32 [4, 4096], P(('groups', 'member'), 'fsdp'), parts along dimension 0
- grad_features: bfloat16 [16, 128, 4096], P(('groups', 'fsdp')), parts along dimension 0
The draws below stay inside these ranges and needn't reach their ends.
There are 2 independent parts, one for each index of `groups`. The reference program is written for one: setup_inputs(seed, part) draws one part's arguments, and reference() takes and returns one part's arrays. A program takes and returns all parts, laid end to end along the dimension named above; an argument that names none is the same for every part. Nothing has to cross between parts.
Inputs may be any that keep to these rules, and one draw needn't show every extreme that they name: `pair_labels`: in every pair the chosen and the rejected entry differ.
All inputs are finite; a program needn't handle non-finite values.
Results may differ from the reference program's by a relative error of at most 0.008.
Values may be sent and summed in bfloat16 or wider, within the bound.
No kernel may reach another device: no remote copies, remote signals or barrier semaphores. Data moves between devices by JAX's collectives and lax.ppermute only.
A program may use at most 256 MiB of HBM per device.

```python
import math
import jax
import jax.numpy as jnp
import numpy as np
from jax import lax

D = 4096
FF = 14336
BLK = 128
LIST = 2
PAIRS = 4
MEMBERS = 2
NBLK = 8


def draw_pair_labels(key, part):
    first_key = jax.random.fold_in(key, 11)
    second_key = jax.random.fold_in(key, 12)
    chosen = jax.random.randint(first_key, (MEMBERS, PAIRS), 0, LIST)
    offset = jax.random.randint(second_key, (MEMBERS, PAIRS), 1, LIST)
    rejected = (chosen + offset) % LIST
    return jnp.stack([chosen, rejected], axis=-1).astype(jnp.int32)


def draw_features(key, part):
    base = jax.random.normal(jax.random.fold_in(key, 21), (NBLK, BLK, D), jnp.float32)
    return jnp.clip(base, -6.0, 6.0).astype(jnp.bfloat16)


def draw_score_head(key, part):
    base = jax.random.normal(jax.random.fold_in(key, 31), (MEMBERS, D), jnp.float32)
    return jnp.clip(0.125 * base, -0.75, 0.75).astype(jnp.float32)


def draw_w_up(key, part):
    base = jnp.clip(jax.random.normal(jax.random.fold_in(key, 41), (MEMBERS, D, FF), jnp.float32), -6.0, 6.0)
    scale = 1.0 / jnp.sqrt(jnp.float32(D))
    return (base * scale).astype(jnp.bfloat16)


def draw_w_down(key, part):
    base = jnp.clip(jax.random.normal(jax.random.fold_in(key, 51), (MEMBERS, FF, D), jnp.float32), -6.0, 6.0)
    scale = 1.0 / jnp.sqrt(jnp.float32(FF))
    return (base * scale).astype(jnp.bfloat16)


def place_ends(array, stream_key, low, top_value):
    spot = [jax.random.randint(jax.random.fold_in(stream_key, axis), (), 0, length) for axis, length in enumerate(array.shape)]
    widest = array.shape.index(max(array.shape))
    beside = spot[:widest] + [(spot[widest] + 1) % array.shape[widest]] + spot[widest + 1:]
    return array.at[tuple(spot)].set(low).at[tuple(beside)].set(top_value)


def level_of(own_key, shape, shards, smallest, largest):
    level = 1.0
    for position, parts in shards:
        draws = jax.random.uniform(jax.random.fold_in(jax.random.fold_in(own_key, 6), position), (parts,), jnp.float32, smallest / len(shards), largest / len(shards))
        level = level * jnp.repeat(jnp.exp(draws), shape[position] // parts).reshape((-1,) + (1,) * (len(shape) - 1 - position))
    return level


def cumulative_ranks(amount, lean):
    weights = [(1 << 20) // math.isqrt(standing ** lean) + 1 for standing in range(1, amount + 1)]
    spread = 1 + sum(weights) // (1 << 30)
    return np.cumsum(np.array([max(1, weight // spread) for weight in weights]))


def ranked_ids(own_key, dims, amount, slope):
    table = cumulative_ranks(amount, slope)
    ticket = jax.random.randint(jax.random.fold_in(own_key, 1), dims, 0, int(table[amount - 1]))
    grade = jnp.searchsorted(jnp.asarray(table, jnp.int32), ticket, side="right")
    return jax.random.permutation(jax.random.fold_in(own_key, 2), amount)[grade].astype(jnp.int32)


def normal_values(stream_key, shape, width, most, split=(), held_as=jnp.bfloat16):
    values = jax.random.normal(stream_key, shape, jnp.float32) * width
    if len(split) > 0:
        values = level_of(stream_key, shape, split, -0.22, 0.18) * values
    return jnp.clip(values, min=-most, max=most).astype(held_as)


def setup_inputs(seed: int = 0, part: int = 0) -> dict:
    arg_keys = jax.random.split(jax.random.key(seed), 10)
    own_keys = jax.random.split(jax.random.fold_in(arg_keys[9], part), 10)
    features = draw_features(jax.random.fold_in(jax.random.fold_in(arg_keys[9], part), 71), part)
    blocks = place_ends(ranked_ids(own_keys[1], (MEMBERS, LIST), NBLK, 2), jax.random.fold_in(own_keys[1], 3), 0, NBLK - 1).astype(jnp.int32)
    pair_labels = draw_pair_labels(jax.random.fold_in(jax.random.fold_in(arg_keys[9], part), 71), part)
    ffn_gain = jnp.clip(jnp.exp(math.log(2.0) - 1.3862944 * jax.random.uniform(arg_keys[3], (MEMBERS, D), jnp.float32) ** level_of(arg_keys[3], (MEMBERS, D), ((0, 2),), -0.2, 0.2)), 0.5, 2.0)
    final_gain = jnp.clip(jnp.exp(math.log(2.0) - 1.3862944 * jax.random.uniform(arg_keys[4], (MEMBERS, D), jnp.float32) ** level_of(arg_keys[4], (MEMBERS, D), ((0, 2),), -0.2, 0.2)), 0.5, 2.0)
    score_head = draw_score_head(jax.random.fold_in(arg_keys[9], 71), part)
    w_gate = normal_values(arg_keys[6], (MEMBERS, D, FF), D ** -0.5, 0.09375, ((0, 2), (2, 8)))
    w_up = draw_w_up(jax.random.fold_in(arg_keys[9], 71), part)
    w_down = draw_w_down(jax.random.fold_in(arg_keys[9], 71), part)
    return {"features": features, "blocks": blocks, "pair_labels": pair_labels, "ffn_gain": ffn_gain, "final_gain": final_gain, "score_head": score_head, "w_gate": w_gate, "w_up": w_up, "w_down": w_down}


eps = 1e-05
loss_scale = 256.0

def pair_terms(scores, pair_rows, entries, block_len):
    reward = lax.optimization_barrier(jnp.mean(scores.reshape(entries, block_len), axis=1))
    slots = jnp.arange(entries, dtype=jnp.int32)
    select = (pair_rows[:, 0:1] == slots[None, :]).astype(jnp.float32) - (pair_rows[:, 1:2] == slots[None, :]).astype(jnp.float32)
    margin = lax.optimization_barrier(jnp.sum(select * reward[None, :], axis=1))
    total_loss = jnp.sum(jax.nn.softplus(-margin))
    weights = -jax.nn.sigmoid(-margin) * loss_scale
    dreward = lax.optimization_barrier(jnp.sum(select * weights[:, None], axis=0))
    dscore = jnp.repeat(dreward / block_len, block_len, total_repeat_length=entries * block_len)
    return (total_loss, dscore)

def contract(left, right, left_dim, right_dim):
    return lax.dot_general(left, right, (((left_dim,), (right_dim,)), ((), ())), preferred_element_type=jnp.float32)

def member_pass(features, chosen_blocks, pair_rows, ffn_gain, final_gain, score_head, w_gate, w_up, w_down):
    entries = chosen_blocks.shape[0]
    block_len = features.shape[1]
    model_width = features.shape[2]
    picked = jnp.take(features, chosen_blocks, axis=0)
    inputs = picked.reshape(entries * block_len, model_width).astype(jnp.float32)
    inverse_in = lax.rsqrt(lax.optimization_barrier(jnp.mean(inputs * inputs, axis=1, keepdims=True)) + eps)
    normed_in = inputs * inverse_in
    scaled_in = (normed_in * ffn_gain[None, :]).astype(jnp.bfloat16)
    gate_pre = jnp.dot(scaled_in, w_gate, preferred_element_type=jnp.float32)
    up_pre = jnp.dot(scaled_in, w_up, preferred_element_type=jnp.float32)
    silu_gate = jax.nn.silu(gate_pre)
    hidden = (silu_gate * up_pre).astype(jnp.bfloat16)
    summed = inputs + jnp.dot(hidden, w_down, preferred_element_type=jnp.float32)
    inverse_out = lax.rsqrt(lax.optimization_barrier(jnp.mean(summed * summed, axis=1, keepdims=True)) + eps)
    normed_out = summed * inverse_out
    gain_head = final_gain * score_head
    scores = lax.optimization_barrier(jnp.sum(normed_out * gain_head[None, :], axis=1))
    total_loss, dscore = pair_terms(scores, pair_rows, entries, block_len)
    weighted = lax.optimization_barrier(jnp.sum(dscore[:, None] * normed_out, axis=0))
    grad_head = final_gain * weighted
    grad_final = score_head * weighted
    dsummed = inverse_out * (dscore[:, None] * gain_head[None, :] - normed_out * (dscore * scores / model_width)[:, None])
    dsummed_b = dsummed.astype(jnp.bfloat16)
    grad_down = contract(hidden, dsummed_b, 0, 0).astype(jnp.bfloat16)
    dhidden = contract(dsummed_b, w_down, 1, 1)
    sigmoid_gate = jax.nn.sigmoid(gate_pre)
    grad_gate_pre = (dhidden * up_pre * sigmoid_gate * (1.0 + gate_pre * (1.0 - sigmoid_gate))).astype(jnp.bfloat16)
    grad_up_pre = (dhidden * silu_gate).astype(jnp.bfloat16)
    grad_gate = contract(scaled_in, grad_gate_pre, 0, 0).astype(jnp.bfloat16)
    grad_up = contract(scaled_in, grad_up_pre, 0, 0).astype(jnp.bfloat16)
    dscaled = contract(grad_gate_pre, w_gate, 1, 1) + contract(grad_up_pre, w_up, 1, 1)
    grad_ffn = lax.optimization_barrier(jnp.sum(dscaled * normed_in, axis=0))
    dnormed_in = dscaled * ffn_gain[None, :]
    drows = inverse_in * (dnormed_in - normed_in * lax.optimization_barrier(jnp.mean(dnormed_in * normed_in, axis=1, keepdims=True))) + dsummed
    drows = drows.astype(jnp.bfloat16).reshape(entries, block_len, model_width)
    owner_hit = (chosen_blocks[None, :] == jnp.arange(features.shape[0], dtype=jnp.int32)[:, None]).astype(jnp.float32)
    per_block = jnp.einsum('kl,lbd->kbd', owner_hit, drows.astype(jnp.float32)).astype(jnp.bfloat16)
    return (total_loss, grad_gate, grad_up, grad_down, grad_head, grad_final, grad_ffn, per_block)

def reference(features, blocks, pair_labels, ffn_gain, final_gain, score_head, w_gate, w_up, w_down):
    results = []
    for member in range(MEMBERS):
        results.append(member_pass(features, blocks[member], pair_labels[member], ffn_gain[member], final_gain[member], score_head[member], w_gate[member], w_up[member], w_down[member]))
    pair_loss = jnp.stack([item[0] for item in results])
    grad_gate = jnp.stack([item[1] for item in results])
    grad_up = jnp.stack([item[2] for item in results])
    grad_down = jnp.stack([item[3] for item in results])
    grad_head = jnp.stack([item[4] for item in results])
    grad_final_gain = jnp.stack([item[5] for item in results])
    grad_ffn_gain = jnp.stack([item[6] for item in results])
    grad_features = jnp.zeros(features.shape, jnp.float32)
    for item in results:
        grad_features = grad_features + item[7].astype(jnp.float32)
    grad_features = grad_features.astype(jnp.bfloat16)
    return (pair_loss, grad_gate, grad_up, grad_down, grad_head, grad_final_gain, grad_ffn_gain, grad_features)
```

```python
import jax
import jax.numpy as jnp
import numpy as np
from jax import lax
from jax.experimental import pallas as pl
from jax.experimental.pallas import tpu as pltpu
from jax.sharding import PartitionSpec as P

eps = 1e-05
loss_scale = 256.0
f32 = jnp.float32
bf16 = jnp.bfloat16


def pair_terms(scores, pair_rows, entries, block_len):
    reward = jnp.mean(scores.reshape(entries, block_len), axis=1)
    slots = jnp.arange(entries, dtype=jnp.int32)
    select = (pair_rows[:, 0:1] == slots[None, :]).astype(f32) - (
        pair_rows[:, 1:2] == slots[None, :]
    ).astype(f32)
    margin = jnp.sum(select * reward[None, :], axis=1)
    total_loss = jnp.sum(jax.nn.softplus(-margin))
    weights = -jax.nn.sigmoid(-margin) * loss_scale
    dreward = jnp.sum(select * weights[:, None], axis=0)
    dscore = jnp.broadcast_to((dreward / block_len)[:, None], (entries, block_len)).reshape(-1)
    return (total_loss, dscore)


def contract(left, right, left_dim, right_dim):
    return lax.dot_general(
        left, right, (((left_dim,), (right_dim,)), ((), ())), preferred_element_type=f32
    )


class Ring:
    def __init__(self, nodes, position):
        order = list(range(0, nodes, 2)) + list(range(nodes - 1, 0, -2))
        self.nodes = nodes
        self.half = nodes // 2
        self.ahead = [(order[i], order[(i + 1) % nodes]) for i in range(nodes)]
        self.back = [(b, a) for a, b in self.ahead]
        place = {device: i for i, device in enumerate(order)}
        table = np.array(
            [[order[(place[d] + k) % nodes] for k in range(nodes)] for d in range(nodes)], np.int32
        )
        self.table = table
        row = lax.dynamic_index_in_dim(jnp.asarray(table), position, 0, keepdims=False)
        self.row = row
        self.device = [row[k] for k in range(nodes)]

    def visited(self, offsets, position):
        return lax.dynamic_index_in_dim(
            jnp.asarray(self.table[:, offsets]), position, 0, keepdims=False
        )

    def up(self, value):
        return lax.ppermute(value, "fsdp", self.ahead)

    def down(self, value):
        return lax.ppermute(value, "fsdp", self.back)

    def gather(self, own, visit):
        from_back = from_ahead = own
        middle = own.shape[0] // 2
        pending = [(0, own)]
        for step in range(1, self.half + 1):
            if step < self.half:
                from_back = self.up(from_back)
                from_ahead = self.down(from_ahead)
                arrived = [(self.nodes - step, from_back), (step, from_ahead)]
            else:
                first = self.up(from_back[:middle])
                second = self.down(from_ahead[middle:])
                arrived = [(step, jnp.concatenate([first, second], axis=0))]
            for offset, band in pending:
                visit(self.device[offset], band)
            pending = arrived
        for offset, band in pending:
            visit(self.device[offset], band)

    def scatter(self, part):
        far = part(self.device[self.half]).astype(bf16)
        middle = far.shape[0] // 2
        first = self.up(far[:middle])
        second = self.down(far[middle:])
        near_up = part(self.device[self.half - 1])
        near_down = part(self.device[self.half + 1])
        going_up = jnp.concatenate(
            [near_up[:middle] + first.astype(f32), near_up[middle:]], axis=0
        ).astype(bf16)
        going_down = jnp.concatenate(
            [near_down[:middle], near_down[middle:] + second.astype(f32)], axis=0
        ).astype(bf16)
        for step in range(self.half - 2, -1, -1):
            going_up = self.up(going_up)
            going_down = self.down(going_down)
            if step:
                going_up = (part(self.device[step]) + going_up.astype(f32)).astype(bf16)
                going_down = (
                    part(self.device[self.nodes - step]) + going_down.astype(f32)
                ).astype(bf16)
        own = part(self.device[0])
        return own + (going_up.astype(f32) + going_down.astype(f32))


def three_terms(value):
    high = lax.reduce_precision(value, 8, 7)
    rest = value - high
    middle = lax.reduce_precision(rest, 8, 7)
    return [term.astype(bf16) for term in (high, middle, rest - middle)]


def to_bands(value, nodes):
    return value.reshape(value.shape[:-1] + (nodes, value.shape[-1] // nodes))


def plain_body(features, blocks, pair_labels, ffn_gain, final_gain, score_head, w_gate, w_up, w_down):
    nodes = lax.axis_size("fsdp")
    position = lax.axis_index("fsdp")
    member = lax.axis_index("member")
    swap = [(0, 1), (1, 0)]
    ring = Ring(nodes, position)
    owned, block_len, width = features.shape
    columns = width // nodes
    half_rows = block_len // 2
    half_columns = columns // 2
    ids = blocks[0]
    entries = ids.shape[0]
    rows = entries * block_len
    w_gate = w_gate[0]
    w_up = w_up[0]
    w_down = w_down[0]
    hidden_count = w_gate.shape[1]
    w_gate_bands = w_gate.reshape(nodes, columns, hidden_count)
    w_up_bands = w_up.reshape(nodes, columns, hidden_count)

    def share(vector, device):
        return lax.dynamic_slice_in_dim(vector, device * columns, columns, 0)

    def down_band(device):
        return lax.dynamic_slice_in_dim(w_down, device * columns, columns, 1)

    other_ids = lax.ppermute(ids, "member", swap)
    sent_rows = lax.dynamic_slice_in_dim(features, member * half_rows, half_rows, 1)
    outgoing = jnp.transpose(to_bands(sent_rows, nodes), (2, 0, 1, 3))
    arrived = lax.all_to_all(outgoing, "fsdp", split_axis=0, concat_axis=0, tiled=True)
    near_half = arrived.reshape(nodes * owned, half_rows, columns)
    far_half = lax.ppermute(near_half, "member", swap)
    picked = jnp.zeros((entries, 2, half_rows, columns), bf16)
    picked = lax.dynamic_update_slice_in_dim(
        picked, jnp.take(near_half, ids, axis=0)[:, None], member, 1
    )
    picked = lax.dynamic_update_slice_in_dim(
        picked, jnp.take(far_half, ids, axis=0)[:, None], 1 - member, 1
    )
    band = picked.reshape(rows, columns)

    stored = features.astype(f32)
    inverse_own = lax.rsqrt(jnp.mean(stored * stored, axis=2) + eps)
    inverse_all = lax.all_gather(inverse_own, "fsdp", axis=0, tiled=True)
    inverse_in = jnp.take(inverse_all, ids, axis=0).reshape(rows, 1)

    gain = ffn_gain[0]
    gain_head = final_gain[0] * score_head[0]
    head_parts = jnp.stack(three_terms(gain_head))
    head_down = jnp.sum(contract(head_parts, w_down, 1, 1), axis=0)

    state = {"gate": None, "up": None, "scaled": jnp.zeros((nodes, rows, columns), bf16)}

    def add(total, value):
        return value if total is None else total + value

    def forward(device, arrived_band):
        scaled = (
            arrived_band.astype(f32) * inverse_in * share(gain, device)[None, :]
        ).astype(bf16)
        gate_band = lax.dynamic_index_in_dim(w_gate_bands, device, 0, keepdims=False)
        up_band = lax.dynamic_index_in_dim(w_up_bands, device, 0, keepdims=False)
        state["gate"] = add(state["gate"], contract(scaled, gate_band, 1, 0))
        state["up"] = add(state["up"], contract(scaled, up_band, 1, 0))
        state["scaled"] = lax.dynamic_update_index_in_dim(state["scaled"], scaled, device, 0)

    ring.gather(band, forward)
    gate_pre = state["gate"]
    up_pre = state["up"]
    sigmoid_gate = jax.nn.sigmoid(gate_pre)
    silu_gate = gate_pre * sigmoid_gate
    hidden = (silu_gate * up_pre).astype(bf16)
    inputs_band = band.astype(f32)
    score_part = jnp.sum(hidden.astype(f32) * head_down[None, :], axis=1) + jnp.sum(
        inputs_band * share(gain_head, position)[None, :], axis=1
    )
    score_parts = lax.all_gather(
        score_part.reshape(1, entries, block_len), "fsdp", axis=0, tiled=True
    )

    out_band = ring.scatter(lambda device: contract(hidden, down_band(device), 1, 0))
    summed_band = inputs_band + out_band

    state2 = {"back": None, "square": None, "summed": jnp.zeros((nodes, rows, columns), bf16)}

    def backward(device, arrived_band):
        wide = arrived_band.astype(f32)
        state2["back"] = add(state2["back"], contract(arrived_band, down_band(device), 1, 1))
        state2["square"] = add(state2["square"], jnp.sum(wide * wide, axis=1))
        state2["summed"] = lax.dynamic_update_index_in_dim(
            state2["summed"], arrived_band, device, 0
        )

    ring.gather(summed_band.astype(bf16), backward)
    inverse_out = lax.rsqrt(state2["square"] / width + eps)
    scores = inverse_out * jnp.sum(score_parts, axis=0).reshape(rows)
    total_loss, dscore = pair_terms(scores, pair_labels[0], entries, block_len)
    head_scale = inverse_out * dscore
    summed_scale = inverse_out * inverse_out * dscore * scores / width
    dhidden = head_scale[:, None] * head_down[None, :] - summed_scale[:, None] * state2["back"]
    grad_gate_pre = (
        dhidden * up_pre * sigmoid_gate * (1.0 + gate_pre * (1.0 - sigmoid_gate))
    ).astype(bf16)
    grad_up_pre = (dhidden * silu_gate).astype(bf16)
    inner_part = jnp.sum(
        grad_gate_pre.astype(f32) * gate_pre + grad_up_pre.astype(f32) * up_pre, axis=1
    )
    inner_parts = lax.all_gather(
        inner_part.reshape(1, entries, block_len), "fsdp", axis=0, tiled=True
    )

    def scaled_part(device):
        gate_band = lax.dynamic_index_in_dim(w_gate_bands, device, 0, keepdims=False)
        up_band = lax.dynamic_index_in_dim(w_up_bands, device, 0, keepdims=False)
        return contract(grad_gate_pre, gate_band, 1, 1) + contract(grad_up_pre, up_band, 1, 1)

    dscaled_band = ring.scatter(scaled_part)

    scaled_in = jnp.transpose(state["scaled"], (1, 0, 2)).reshape(rows, width)
    summed = jnp.transpose(state2["summed"], (1, 0, 2)).reshape(rows, width)
    dsummed_b = (
        head_scale[:, None] * gain_head[None, :] - summed_scale[:, None] * summed.astype(f32)
    ).astype(bf16)
    grad_gate = contract(scaled_in, grad_gate_pre, 0, 0).astype(bf16)
    grad_up = contract(scaled_in, grad_up_pre, 0, 0).astype(bf16)
    grad_down = contract(hidden, dsummed_b, 0, 0).astype(bf16)

    weighted = jnp.sum(head_scale[:, None] * summed_band, axis=0)
    grad_head = share(final_gain[0], position) * weighted
    grad_final = share(score_head[0], position) * weighted
    dsummed_band = (
        head_scale[:, None] * share(gain_head, position)[None, :]
        - summed_scale[:, None] * summed_band
    )

    normed_in_band = inputs_band * inverse_in
    grad_ffn = jnp.sum(dscaled_band * normed_in_band, axis=0)
    row_inner = jnp.sum(inner_parts, axis=0).reshape(rows, 1)
    drows = (
        inverse_in
        * (dscaled_band * share(gain, position)[None, :] - normed_in_band * (row_inner / width))
        + dsummed_band
    ).astype(bf16)

    kept = lax.dynamic_slice_in_dim(drows, member * half_columns, half_columns, 1)
    given = lax.dynamic_slice_in_dim(drows, (1 - member) * half_columns, half_columns, 1)
    taken = lax.ppermute(given, "member", swap)

    def by_block(listed, value):
        hit = listed[None, :] == jnp.arange(nodes * owned, dtype=jnp.int32)[:, None]
        value = value.reshape(entries, block_len, half_columns).astype(f32)
        total = sum(
            jnp.where(hit[:, entry, None, None], value[entry][None], 0.0)
            for entry in range(entries)
        )
        return total.astype(bf16).astype(f32)

    returned = (by_block(ids, kept) + by_block(other_ids, taken)).astype(bf16)
    returned = returned.reshape(nodes, owned, block_len, half_columns)
    mine = lax.all_to_all(returned, "fsdp", split_axis=0, concat_axis=0, tiled=True)
    other = lax.ppermute(mine, "member", swap)
    whole = jnp.zeros((2, nodes, owned, block_len, half_columns), bf16)
    whole = lax.dynamic_update_index_in_dim(whole, mine, member, 0)
    whole = lax.dynamic_update_index_in_dim(whole, other, 1 - member, 0)
    grad_features = jnp.transpose(whole, (2, 3, 1, 0, 4)).reshape(owned, block_len, width)
    return (
        total_loss.reshape(1),
        grad_gate[None],
        grad_up[None],
        grad_down[None],
        grad_head[None],
        grad_final[None],
        grad_ffn[None],
        grad_features,
    )


AUX = 16
STRIPE = 32
IN_SMEM = pl.BlockSpec(memory_space=pltpu.SMEM)
IN_VMEM = pl.BlockSpec(memory_space=pltpu.VMEM)
IN_HBM = pl.BlockSpec(memory_space=pltpu.HBM)


def dot(left, right, left_dim, right_dim):
    return contract(left, right, left_dim, right_dim)


def call(kernel, operands, specs, outs, scratch=(), limit=8, aliases=None):
    operands = [
        pltpu.with_memory_space_constraint(value, pltpu.HBM) if spec is IN_HBM else value
        for value, spec in zip(operands, specs)
    ]
    return pl.pallas_call(
        kernel,
        out_shape=[jax.ShapeDtypeStruct(shape, dtype) for shape, dtype in outs],
        in_specs=specs,
        scratch_shapes=list(scratch),
        input_output_aliases=aliases or {},
        compiler_params=pltpu.CompilerParams(vmem_limit_bytes=limit << 20),
    )(*operands)


def band_number(row_ref, offsets, k):
    if len(offsets) == 1:
        return row_ref[offsets[0]]
    return row_ref[offsets[0] + k * (offsets[1] - offsets[0])]


def stream(count, sources, weights, done, use):
    ways = len(sources)

    def copy(k, w):
        slot = k * ways + w
        return pltpu.make_async_copy(sources[w](k), weights.at[slot], done.at[slot])

    for w in range(ways):
        copy(0, w).start()

    def step(k):
        for w in range(ways):
            copy(k, w).wait()
            if isinstance(k, int):
                if k + 1 < count:
                    copy(k + 1, w).start()
            else:

                @pl.when(k + 1 < count)
                def _():
                    copy(k + 1, w).start()

            use(k, w, weights.at[k * ways + w])

    if count == 1:
        return lambda: step(0)

    def run():
        def body(k, _):
            step(k)
            return 0

        lax.fori_loop(0, count, body, 0)

    return run


def rows_as_lanes(vectors):
    rows = vectors[0].shape[0]
    lane = lax.broadcasted_iota(jnp.int32, (rows, 128), 1)
    packed = jnp.zeros((rows, 128), f32)
    for k, vector in enumerate(vectors):
        packed = jnp.where(lane == k, vector, packed)
    return packed.T[:8]


def lanes_as_columns(vectors):
    rows = vectors[0].shape[1]
    line = lax.broadcasted_iota(jnp.int32, (128, rows), 0)
    packed = jnp.zeros((128, rows), f32)
    for k, vector in enumerate(vectors):
        packed = jnp.where(line == k, vector, packed)
    return packed.T


def split_terms(lanes):
    high = lanes.astype(bf16).astype(f32)
    rest = lanes - high
    middle = rest.astype(bf16).astype(f32)
    low = rest - middle
    top = jnp.concatenate([high, middle], axis=1)
    bottom = jnp.concatenate([low, jnp.zeros_like(low)], axis=1)
    return jnp.concatenate([top, bottom], axis=0).astype(bf16)


def joined_term(terms, k):
    half = terms.shape[1] // 2
    return terms[k : k + 1, :half] + terms[k : k + 1, half:] + terms[8 + k : 9 + k, :half]


def pieces_of(band):
    return band if isinstance(band, tuple) else (band,)


def pack_blocks(member, block, nodes):
    block_len, width = block.shape
    columns = width // nodes
    half = columns // 2

    def kernel(member_ref, block_ref, out):
        square = jnp.zeros((block_len, 1), f32)
        for d in range(nodes):
            part = block_ref[:, d * columns : (d + 1) * columns].astype(f32)
            square += jnp.sum(part * part, axis=1, keepdims=True)
        terms = split_terms(rows_as_lanes([lax.rsqrt(square / width + eps)]))
        for d in range(nodes):
            start = pl.multiple_of(d * columns + member_ref[0] * half, half)
            out[d, :block_len] = block_ref[:, pl.ds(start, half)]
            out[d, block_len:] = terms

    return call(
        kernel, [member, block], [IN_SMEM, IN_VMEM], [((nodes, block_len + AUX, half), bf16)]
    )[0]


def pick_blocks(ids, member, near, far):
    entries = ids.shape[0]
    block_len = near.shape[1] - AUX
    half = near.shape[2]

    def kernel(ids_ref, member_ref, near_ref, far_ref, band_out, inverse_out):
        first = member_ref[0] == 0
        for e in range(entries):
            mine, other = near_ref[ids_ref[e]], far_ref[ids_ref[e]]
            part = slice(e * block_len, (e + 1) * block_len)
            band_out[part, :half] = jnp.where(first, mine, other)[:block_len]
            band_out[part, half:] = jnp.where(first, other, mine)[:block_len]
            row = joined_term(mine[block_len:].astype(f32), 0)
            inverse_out[part] = lanes_as_columns([row])[:, 0:1]

    return call(
        kernel, [ids, member, near, far], [IN_SMEM, IN_SMEM, IN_VMEM, IN_VMEM],
        [((entries * block_len, 2 * half), bf16), ((entries * block_len, 1), f32)],
    )


def split_halves(back, ahead, middle):
    def kernel(back_ref, ahead_ref, first, second):
        first[...] = back_ref[:middle]
        second[...] = ahead_ref[middle:]

    columns = back.shape[1]
    return call(
        kernel, [back, ahead], [IN_VMEM] * 2,
        [((middle, columns), bf16), ((ahead.shape[0] - middle, columns), bf16)],
    )


def forward_bands(bands, row, offsets, gain_bands, inverse, gate_bands, up_bands, totals, head):
    bands = [pieces_of(band) for band in bands]
    flat = [piece for band in bands for piece in band]
    count = len(bands)
    rows, columns = inverse.shape[0], flat[0].shape[1]
    width = gate_bands.shape[2]
    last = head is not None

    def kernel(row_ref, *refs):
        refs = list(refs)
        take = lambda k: [refs.pop(0) for _ in range(k)]
        band_refs = [take(len(band)) for band in bands]
        gain_ref, inverse_ref, gate_hbm, up_hbm = take(4)
        if totals:
            take(2)
        head_ref = take(1)[0] if last else None
        totals_out = take(2)
        (scaled_out,) = take(1)
        hidden_out, score_out = take(2) if last else (None, None)
        weights, done = refs

        def use(k, w, block):
            totals_out[w][...] += dot(scaled_out[k], block[...], 1, 0)

        run = stream(
            count,
            [
                lambda k: gate_hbm.at[band_number(row_ref, offsets, k)],
                lambda k: up_hbm.at[band_number(row_ref, offsets, k)],
            ],
            weights, done, use,
        )
        for k in range(count):
            start = 0
            for ref in band_refs[k]:
                part = slice(start, start + ref.shape[0])
                scaled_out[k, part] = (
                    ref[...].astype(f32) * inverse_ref[part] * gain_ref[row_ref[offsets[k]]]
                ).astype(bf16)
                start += ref.shape[0]
        if not totals:
            for out in totals_out:
                out[...] = jnp.zeros_like(out)
        run()
        if last:
            gate_out, up_out = totals_out

            def finish(i, _):
                part = pl.ds(i * STRIPE, STRIPE)
                gate = gate_out[part]
                hidden = (gate * jax.nn.sigmoid(gate) * up_out[part]).astype(bf16)
                hidden_out[part] = hidden
                score_out[part] = jnp.sum(
                    hidden.astype(f32) * head_ref[...], axis=1, keepdims=True
                )
                return 0

            lax.fori_loop(0, rows // STRIPE, finish, 0)

    operands = [row] + flat + [gain_bands, inverse, gate_bands, up_bands]
    specs = [IN_SMEM] + [IN_VMEM] * (len(flat) + 2) + [IN_HBM, IN_HBM]
    aliases = {}
    if totals:
        aliases = {len(operands): 0, len(operands) + 1: 1}
        operands += list(totals)
        specs += [IN_VMEM] * 2
    if last:
        operands.append(head)
        specs.append(IN_VMEM)
    outs = [((rows, width), f32)] * 2 + [((count, rows, columns), bf16)]
    if last:
        outs += [((rows, width), bf16), ((rows, 1), f32)]
    scratch = [
        pltpu.VMEM((2 * count, columns, width), bf16), pltpu.SemaphoreType.DMA((2 * count,))
    ]
    out = call(kernel, operands, specs, outs, scratch, 8 + 4 * count, aliases)
    return out[:2], out[2], out[3:]


def pair_scales(notes, labels_ref, rows, entries, width):
    square, score = joined_term(notes, 0), joined_term(notes, 1)
    inverse_out = lax.rsqrt(square / width + eps)
    scores = inverse_out * score
    block_len = rows // entries
    rewards = [
        jnp.sum(scores[:, e * block_len : (e + 1) * block_len], axis=1, keepdims=True) / block_len
        for e in range(entries)
    ]
    drewards = [jnp.zeros((1, 1), f32) for _ in range(entries)]
    loss = jnp.zeros((1, 1), f32)
    for p in range(labels_ref.shape[0]):
        select = [
            (labels_ref[p, 0] == e).astype(f32) - (labels_ref[p, 1] == e).astype(f32)
            for e in range(entries)
        ]
        margin = sum(select[e] * rewards[e] for e in range(entries))
        loss += jnp.maximum(-margin, 0.0) + jnp.log1p(jnp.exp(-jnp.abs(margin)))
        weight = -jax.nn.sigmoid(-margin) * loss_scale
        drewards = [drewards[e] + select[e] * weight for e in range(entries)]
    lane = lax.broadcasted_iota(jnp.int32, (1, rows), 1)
    dscore = jnp.zeros((1, rows), f32)
    for e in range(entries):
        dscore = jnp.where(lane // block_len == e, drewards[e] / block_len, dscore)
    head_scale = inverse_out * dscore
    columns = lanes_as_columns([head_scale, inverse_out * head_scale * scores / width])
    return loss, columns[:, 0:1], columns[:, 1:2]


def backward_bands(bands, row, offsets, w_down, rows, total, final):
    bands = [pieces_of(band) for band in bands]
    flat = [piece for band in bands for piece in band]
    count = len(bands)
    columns = flat[0].shape[1]
    width, model_width = w_down.shape
    others = final[4] if final else []

    def kernel(row_ref, *refs):
        refs = list(refs)
        take = lambda k: [refs.pop(0) for _ in range(k)]
        band_refs = [take(len(band)) for band in bands]
        (down_hbm,) = take(1)
        if total is not None:
            take(1)
        if final:
            gate_ref, up_ref, head_ref, labels_ref = take(4)
            other_refs = take(len(others))
        (back_ref,) = take(1)
        if final:
            grads_out, inner_out, loss_out, head_scale, summed_scale = take(5)
        weights, done, kept = take(3)

        def use(k, w, block):
            back_ref[...] += dot(kept[k], block[...], 1, 1)

        def source(k):
            start = pl.multiple_of(band_number(row_ref, offsets, k) * columns, columns)
            return down_hbm.at[:, pl.ds(start, columns)]

        run = stream(count, [source], weights, done, use)
        for k in range(count):
            start = 0
            for ref in band_refs[k]:
                size = min(ref.shape[0], rows - start)
                kept[k, start : start + size] = ref[:size]
                start += size
        if total is None:
            back_ref[...] = jnp.zeros_like(back_ref)
        if final:
            tail = band_refs[-1][-1]
            notes = tail[tail.shape[0] - AUX :].astype(f32)
            for ref in other_refs:
                notes += ref[rows:].astype(f32)
            loss, head_column, summed_column = pair_scales(
                notes, labels_ref, rows, final[5], model_width
            )
            loss_out[...] = loss
            head_scale[...] = head_column
            summed_scale[...] = summed_column
        run()
        if not final:
            return
        (inner,) = refs

        def finish(i, _):
            part = pl.ds(i * STRIPE, STRIPE)
            gate, up = gate_ref[part], up_ref[part]
            sigmoid = jax.nn.sigmoid(gate)
            dhidden = head_scale[part] * head_ref[...] - summed_scale[part] * back_ref[part]
            dgate = (dhidden * up * sigmoid * (1.0 + gate * (1.0 - sigmoid))).astype(bf16)
            dup = (dhidden * (gate * sigmoid)).astype(bf16)
            grads_out[0, part] = dgate
            grads_out[1, part] = dup
            inner[part] = jnp.sum(
                dgate.astype(f32) * gate + dup.astype(f32) * up, axis=1, keepdims=True
            )
            return 0

        lax.fori_loop(0, rows // STRIPE, finish, 0)
        inner_out[...] = rows_as_lanes([inner[...]])

    operands = [row] + flat + [w_down]
    specs = [IN_SMEM] + [IN_VMEM] * len(flat) + [IN_HBM]
    aliases = {}
    if total is not None:
        aliases = {len(operands): 0}
        operands.append(total)
        specs.append(IN_VMEM)
    scratch = [
        pltpu.VMEM((count, width, columns), bf16), pltpu.SemaphoreType.DMA((count,)),
        pltpu.VMEM((count, rows, columns), bf16),
    ]
    outs = [((rows, width), f32)]
    if final:
        operands += list(final[:4]) + list(others)
        specs += [IN_VMEM] * 3 + [IN_SMEM] + [IN_VMEM] * len(others)
        outs += [
            ((2, rows, width), bf16), ((8, rows), f32), ((1, 1), f32), ((rows, 1), f32),
            ((rows, 1), f32),
        ]
        scratch += [pltpu.VMEM((rows, 1), f32)]
    return call(kernel, operands, specs, outs, scratch, 8 + 3 * count, aliases)


def out_parts(row, offsets, hidden, w_down, columns):
    count = len(offsets)
    rows, width = hidden.shape

    def kernel(row_ref, hidden_ref, down_hbm, out, weights, done):
        def use(k, w, block):
            out[k] = dot(hidden_ref[...], block[...], 1, 0)

        def source(k):
            start = pl.multiple_of(band_number(row_ref, offsets, k) * columns, columns)
            return down_hbm.at[:, pl.ds(start, columns)]

        stream(count, [source], weights, done, use)()

    return call(
        kernel, [row, hidden, w_down], [IN_SMEM, IN_VMEM, IN_HBM],
        [((count, rows, columns), f32)],
        [pltpu.VMEM((count, width, columns), bf16), pltpu.SemaphoreType.DMA((count,))],
        4 + 3 * count,
    )[0]


def scaled_parts(row, offsets, grads, gate_bands, up_bands):
    count = len(offsets)
    rows, width = grads.shape[1:]
    columns = gate_bands.shape[1]

    def kernel(row_ref, grads_ref, gate_hbm, up_hbm, out, weights, done):
        def use(k, w, block):
            term = dot(grads_ref[w], block[...], 1, 1)
            if w:
                out[k] += term
            else:
                out[k] = term

        stream(
            count,
            [
                lambda k: gate_hbm.at[band_number(row_ref, offsets, k)],
                lambda k: up_hbm.at[band_number(row_ref, offsets, k)],
            ],
            weights, done, use,
        )()

    return call(
        kernel, [row, grads, gate_bands, up_bands], [IN_SMEM, IN_VMEM, IN_HBM, IN_HBM],
        [((count, rows, columns), f32)],
        [pltpu.VMEM((2 * count, columns, width), bf16), pltpu.SemaphoreType.DMA((2 * count,))],
        4 + 5 * count,
    )[0]


def high_low(row):
    high = row.astype(bf16).astype(f32)
    return jnp.concatenate([high, row - high], axis=1)


def add_arrivals(parts, from_back, from_ahead, inner):
    rows, columns = parts.shape[1:]
    middle = rows // 2
    tail = 0 if inner is None else AUX
    early = from_back.shape[0] < rows

    def kernel(*refs):
        parts_ref, back_ref, ahead_ref = refs[:3]
        out_up, out_down = refs[-2:]
        if early:
            out_up[:middle] = (parts_ref[0, :middle] + back_ref[:middle].astype(f32)).astype(bf16)
            out_up[middle:rows] = parts_ref[0, middle:].astype(bf16)
            out_down[:middle] = parts_ref[1, :middle].astype(bf16)
            out_down[middle:rows] = (
                parts_ref[1, middle:] + ahead_ref[:middle].astype(f32)
            ).astype(bf16)
        else:
            out_up[:rows] = (parts_ref[0] + back_ref[:rows].astype(f32)).astype(bf16)
            out_down[:rows] = (parts_ref[1] + ahead_ref[:rows].astype(f32)).astype(bf16)
        if tail:
            row = refs[3][...]
            base = middle if early else rows
            pad = jnp.zeros((AUX - 8, columns), f32)

            def carry(ref):
                came = ref[base:].astype(f32)[:8]
                return row + came[:, : columns // 2] + came[:, columns // 2 :]

            up_row = carry(back_ref)
            down_row = row if early else carry(ahead_ref)
            out_up[rows:] = jnp.concatenate([high_low(up_row), pad], axis=0).astype(bf16)
            out_down[rows:] = jnp.concatenate([high_low(down_row), pad], axis=0).astype(bf16)

    operands = [parts, from_back, from_ahead] + ([] if inner is None else [inner])
    return call(
        kernel, operands, [IN_VMEM] * len(operands), [((rows + tail, columns), bf16)] * 2
    )


def first_messages(far, inner):
    rows, columns = far.shape[1:]
    middle = rows // 2
    tail = 0 if inner is None else AUX

    def kernel(far_ref, *refs):
        up_out, down_out = refs[-2:]
        up_out[:middle] = far_ref[0, :middle].astype(bf16)
        down_out[...] = far_ref[0, middle:].astype(bf16)
        if tail:
            pad = jnp.zeros((AUX - 8, columns), f32)
            up_out[middle:] = jnp.concatenate([high_low(refs[0][...]), pad], axis=0).astype(bf16)

    operands = [far] + ([] if inner is None else [inner])
    return call(
        kernel, operands, [IN_VMEM] * len(operands),
        [((middle + tail, columns), bf16), ((middle, columns), bf16)],
    )


def finish_summed(own, from_back, from_ahead, band, head_row, score):
    rows, columns = own.shape[1:]

    def kernel(own_ref, back_ref, ahead_ref, band_ref, head_ref, score_ref, summed_out, message):
        inputs = band_ref[...].astype(f32)
        summed = inputs + (
            own_ref[0] + (back_ref[...].astype(f32) + ahead_ref[...].astype(f32))
        )
        summed_out[...] = summed
        message[:rows] = summed.astype(bf16)
        square = jnp.sum(summed * summed, axis=1, keepdims=True)
        share = score_ref[...] + jnp.sum(inputs * head_ref[...], axis=1, keepdims=True)
        message[rows:] = split_terms(rows_as_lanes([square, share]))

    return call(
        kernel, [own, from_back, from_ahead, band, head_row, score], [IN_VMEM] * 6,
        [((rows, columns), f32), ((rows + AUX, columns), bf16)],
    )


def finish_rows(member, own, from_back, from_ahead, inner, band, summed, inverse, gain_row,
                head_row, head_scale, summed_scale, final_row, score_row, entries, width):
    rows, columns = own.shape[1:]
    block_len = rows // entries
    half = block_len // 2

    def kernel(member_ref, own_ref, back_ref, ahead_ref, inner_ref, band_ref, summed_ref,
               inverse_ref, gain_ref, head_ref, head_scale_ref, summed_scale_ref, final_ref,
               score_ref, kept_out, given_out, ffn_out, head_out, final_out, drows):
        dscaled = own_ref[0] + (back_ref[:rows].astype(f32) + ahead_ref[:rows].astype(f32))
        came = (back_ref[rows:].astype(f32) + ahead_ref[rows:].astype(f32))[:8]
        lanes = inner_ref[...] + came[:, : columns // 2] + came[:, columns // 2 :]
        inner_column = lanes_as_columns([lanes[0:1]])[:, 0:1]
        inverse_in = inverse_ref[...]
        normed = band_ref[...].astype(f32) * inverse_in
        ffn_out[...] = jnp.sum(dscaled * normed, axis=0, keepdims=True)
        summed = summed_ref[...]
        weighted = jnp.sum(head_scale_ref[...] * summed, axis=0, keepdims=True)
        head_out[...] = final_ref[...] * weighted
        final_out[...] = score_ref[...] * weighted
        dsummed = head_scale_ref[...] * head_ref[...] - summed_scale_ref[...] * summed
        drows[...] = (
            inverse_in * (dscaled * gain_ref[...] - normed * (inner_column / width)) + dsummed
        ).astype(bf16)
        for e in range(entries):
            for out, which in ((kept_out, member_ref[0]), (given_out, 1 - member_ref[0])):
                start = pl.multiple_of(e * block_len + which * half, half)
                out[e] = drows[pl.ds(start, half)]

    return call(
        kernel,
        [member, own, from_back, from_ahead, inner, band, summed, inverse, gain_row, head_row,
         head_scale, summed_scale, final_row, score_row],
        [IN_SMEM] + [IN_VMEM] * 13,
        [((entries, half, columns), bf16)] * 2 + [((1, columns), f32)] * 3,
        [pltpu.VMEM((rows, columns), bf16)],
    )


def route_rows(ids, other_ids, kept, taken, blocks):
    entries, half, columns = kept.shape

    def kernel(ids_ref, other_ref, kept_ref, taken_ref, out):
        for b in range(blocks):
            sums = []
            for listed, value in ((ids_ref, kept_ref), (other_ref, taken_ref)):
                total = jnp.zeros((half, columns), f32)
                for e in range(entries):
                    total += jnp.where(listed[e] == b, value[e].astype(f32), 0.0)
                sums.append(total.astype(bf16).astype(f32))
            out[b] = (sums[0] + sums[1]).astype(bf16)

    return call(
        kernel, [ids, other_ids, kept, taken], [IN_SMEM, IN_SMEM, IN_VMEM, IN_VMEM],
        [((blocks, half, columns), bf16)],
    )[0]


def assemble_block(member, mine, other):
    nodes, half, columns = mine.shape

    def kernel(member_ref, mine_ref, other_ref, out):
        for value, which in ((mine_ref, member_ref[0]), (other_ref, 1 - member_ref[0])):
            part = pl.ds(pl.multiple_of(which * half, half), half)
            for d in range(nodes):
                out[part, d * columns : (d + 1) * columns] = value[d]

    return call(
        kernel, [member, mine, other], [IN_SMEM, IN_VMEM, IN_VMEM],
        [((2 * half, nodes * columns), bf16)],
    )[0]


def turned(value):
    def kernel(value_ref, out):
        out[...] = value_ref[...].T

    return call(kernel, [value], [IN_VMEM], [(value.shape[::-1], value.dtype)])[0]


def whole(*shape):
    zeros = (0,) * len(shape)
    return pl.BlockSpec(shape, lambda *_: zeros)


def grid_call(kernel, index, operands, specs, outs, out_specs, steps, scratch, aliases=None):
    return pl.pallas_call(
        kernel,
        out_shape=[jax.ShapeDtypeStruct(shape, dtype) for shape, dtype in outs],
        grid_spec=pltpu.PrefetchScalarGridSpec(
            num_scalar_prefetch=1, grid=(steps,), in_specs=specs, out_specs=out_specs,
            scratch_shapes=list(scratch),
        ),
        input_output_aliases=aliases or {},
        compiler_params=pltpu.CompilerParams(vmem_limit_bytes=20 << 20),
    )(index, *operands)


def weight_grads(index, stacks, grads):
    nodes = sum(stack.shape[0] for stack in stacks)
    _, rows, columns = stacks[0].shape
    width = grads.shape[2]

    def kernel(index_ref, *refs):
        grads_ref, gate_out, up_out, kept = refs[len(stacks) :]

        @pl.when(pl.program_id(0) == 0)
        def _():
            start = 0
            for ref in refs[: len(stacks)]:
                kept[start : start + ref.shape[0]] = ref[...]
                start += ref.shape[0]

        scaled = kept[pl.program_id(0)].T
        gate_out[0] = dot(scaled, grads_ref[0], 1, 0).astype(bf16)
        up_out[0] = dot(scaled, grads_ref[1], 1, 0).astype(bf16)

    out = pl.BlockSpec((1, columns, width), lambda b, idx: (idx[b], 0, 0))
    return grid_call(
        kernel, index, list(stacks) + [grads], [IN_VMEM] * (len(stacks) + 1),
        [((nodes, columns, width), bf16)] * 2, [out, out], nodes,
        [pltpu.VMEM((nodes, rows, columns), bf16)],
    )


def down_grad(index, start, bands, hidden_t, head_bands, head_scale, summed_scale, before):
    flat = [piece for band in bands for piece in pieces_of(band)]
    columns = flat[0].shape[1]
    width, rows = hidden_t.shape
    nodes = head_bands.shape[0]

    def kernel(index_ref, *refs):
        hidden_ref, head_ref, head_scale_ref, summed_scale_ref = refs[len(flat) : len(flat) + 4]
        out, kept = refs[-2:]

        @pl.when(pl.program_id(0) == 0)
        def _():
            at = 0
            for k, band in enumerate(bands):
                line = 0
                for _ in pieces_of(band):
                    size = min(refs[at].shape[0], rows - line)
                    kept[k, line : line + size] = refs[at][:size]
                    line += size
                    at += 1

        step = pl.program_id(0)
        dsummed = (
            head_scale_ref[...] * head_ref[index_ref[start + step]]
            - summed_scale_ref[...] * kept[step].astype(f32)
        )
        out[...] = dot(hidden_ref[...], dsummed.astype(bf16), 1, 0).astype(bf16)

    operands = flat + [hidden_t, head_bands, head_scale, summed_scale]
    specs = [IN_VMEM] * len(operands)
    aliases = None
    if before is not None:
        aliases = {len(operands) + 1: 0}
        operands.append(before)
        specs.append(pl.BlockSpec(memory_space=pl.ANY))
    return grid_call(
        kernel, index, operands, specs, [((width, nodes * columns), bf16)],
        [pl.BlockSpec((width, columns), lambda b, idx: (0, idx[start + b]))], len(bands),
        [pltpu.VMEM((len(bands), rows, columns), bf16)], aliases,
    )[0]


def after(values, *others):
    return lax.optimization_barrier(tuple(values) + tuple(others))[: len(values)]


def ring_body(features, blocks, pair_labels, ffn_gain, final_gain, score_head, w_gate, w_up, w_down):
    nodes = lax.axis_size("fsdp")
    position = lax.axis_index("fsdp")
    member = lax.axis_index("member").reshape(1)
    swap = [(0, 1), (1, 0)]
    ring = Ring(nodes, position)
    half = ring.half
    block_len, width = features.shape[1:]
    columns = width // nodes
    ids = blocks[0]
    entries = ids.shape[0]
    rows = entries * block_len
    middle = rows // 2
    w_gate = w_gate[0]
    w_up = w_up[0]
    w_down = w_down[0]
    hidden_count = w_gate.shape[1]
    gate_bands = w_gate.reshape(nodes, columns, hidden_count)
    up_bands = w_up.reshape(nodes, columns, hidden_count)
    gain_head = final_gain[0] * score_head[0]
    gain_bands = ffn_gain.reshape(nodes, 1, columns)
    head_bands = gain_head.reshape(nodes, 1, columns)

    def share(vector):
        return lax.dynamic_slice_in_dim(vector, position * columns, columns, 0)[None]

    other_ids = lax.ppermute(ids, "member", swap)
    sent = pack_blocks(member, features[0], nodes)
    near = lax.all_to_all(sent, "fsdp", split_axis=0, concat_axis=0, tiled=True)
    head_parts = jnp.stack(three_terms(gain_head))
    head_down = jnp.sum(contract(head_parts, w_down, 1, 1), axis=0)[None]
    (near,) = after([near], head_down)
    far = lax.ppermute(near, "member", swap)
    band, inverse_in = pick_blocks(ids, member, near, far)

    def gather(own, visit, extra=None):
        back = ahead = own
        total = None
        pending, pending_offsets = [own], [0]
        order = []
        for step in range(1, half + 1):
            if step < half:
                back, ahead = ring.up(back), ring.down(ahead)
                arrived, offsets = [back, ahead], [nodes - step, step]
            else:
                first, second = split_halves(back, ahead, middle)
                arrived, offsets = [(ring.up(first), ring.down(second))], [step]
            total = visit(pending, pending_offsets, total)
            order += pending_offsets
            if step < half:
                done = list(total)
                if step == 1 and extra is not None:
                    done.append(extra)
                back, ahead = after([back, ahead], *done)
                arrived = [back, ahead]
            pending, pending_offsets = arrived, offsets
        order += pending_offsets
        return pending, pending_offsets, total, order

    scaled = []

    def forward(bands, offsets, total, head=None):
        total, new, rest = forward_bands(
            bands, ring.row, offsets, gain_bands, inverse_in, gate_bands, up_bands, total, head
        )
        scaled.append(new)
        return total if head is None else (total, rest)

    last, last_offsets, total, offsets = gather(band, forward)
    order = ring.visited(offsets, position)
    (gate_pre, up_pre), (hidden, score) = forward(last, last_offsets, total, head_down)

    far_part = out_parts(ring.row, [half], hidden, w_down, columns)
    up_message, down_message = first_messages(far_part, None)
    (held,) = after([hidden], up_message)
    back, ahead = ring.up(up_message), ring.down(down_message)
    for step in range(half - 1, 0, -1):
        parts = out_parts(ring.row, [step, nodes - step], held, w_down, columns)
        (held,) = after([held], back, ahead)
        back, ahead = add_arrivals(parts, back, ahead, None)
        back, ahead = ring.up(back), ring.down(ahead)
    own_part = out_parts(ring.row, [0], held, w_down, columns)
    summed_band, message = finish_summed(
        own_part, back, ahead, band, share(gain_head), score
    )

    messages = []

    def backward(bands, offsets, total, final=None):
        messages.extend(bands)
        return backward_bands(
            bands, ring.row, offsets, w_down, rows, None if total is None else total[0], final
        )

    (held,) = after([hidden], message)
    hidden_t = turned(held)
    last, last_offsets, total, _ = gather(message, backward, hidden_t)
    _, grads, inner, loss, head_scale, summed_scale = backward(
        last, last_offsets, total,
        (gate_pre, up_pre, head_down, pair_labels[0], list(messages), entries),
    )

    far_part = scaled_parts(ring.row, [half], grads, gate_bands, up_bands)
    up_message, down_message = first_messages(far_part, inner)
    (held,) = after([grads], up_message)
    back, ahead = ring.up(up_message), ring.down(down_message)
    grad_down = None
    bounds = [0, 3, 6, nodes]

    def grad_down_piece(piece, held_t):
        start, stop = bounds[piece], bounds[piece + 1]
        return down_grad(
            order, start, messages[start:stop], held_t, head_bands, head_scale, summed_scale,
            grad_down,
        )

    for step in range(half - 1, 0, -1):
        parts = scaled_parts(ring.row, [step, nodes - step], held, gate_bands, up_bands)
        if step < half - 1:
            grad_down = grad_down_piece(half - 2 - step, hidden_t)
            back, ahead = after([back, ahead], grad_down)
        held, hidden_t = after([held, hidden_t], back, ahead)
        back, ahead = add_arrivals(parts, back, ahead, inner)
        back, ahead = ring.up(back), ring.down(ahead)
    own_part = scaled_parts(ring.row, [0], held, gate_bands, up_bands)
    grad_down = grad_down_piece(2, hidden_t)
    back, ahead = after([back, ahead], grad_down)
    kept, given, grad_ffn, grad_head, grad_final = finish_rows(
        member, own_part, back, ahead, inner, band, summed_band, inverse_in,
        share(ffn_gain[0]), share(gain_head), head_scale, summed_scale, share(final_gain[0]),
        share(score_head[0]), entries, width,
    )

    (held,) = after([grads], given)
    taken = lax.ppermute(given, "member", swap)
    returned = route_rows(ids, other_ids, kept, taken, nodes)
    mine = lax.all_to_all(returned, "fsdp", split_axis=0, concat_axis=0, tiled=True)
    grad_gate, grad_up = weight_grads(order, scaled, held)
    (mine,) = after([mine], grad_gate, grad_up)
    other = lax.ppermute(mine, "member", swap)
    grad_features = assemble_block(member, mine, other)
    return (
        loss.reshape(1),
        grad_gate.reshape(1, width, hidden_count),
        grad_up.reshape(1, width, hidden_count),
        grad_down[None],
        grad_head,
        grad_final,
        grad_ffn,
        grad_features[None],
    )


def body(features, blocks, pair_labels, ffn_gain, final_gain, score_head, w_gate, w_up, w_down):
    nodes = lax.axis_size("fsdp")
    rows = blocks.shape[1] * features.shape[1]
    columns = features.shape[2] // nodes
    tiled = w_gate.shape[2] % 256 == 0 and columns == 2 * rows and rows % 256 == 0
    single = features.shape[0] == 1 and lax.axis_size("member") == 2
    chosen = ring_body if tiled and single and nodes == 8 else plain_body
    return chosen(
        features, blocks, pair_labels, ffn_gain, final_gain, score_head, w_gate, w_up, w_down
    )


def solution(mesh):
    in_specs = (
        P(("groups", "fsdp"), None, None),
        P(("groups", "member"), None),
        P(("groups", "member"), None, None),
        P("member", None),
        P("member", None),
        P("member", None),
        P("member", None, "fsdp"),
        P("member", None, "fsdp"),
        P("member", "fsdp", None),
    )
    out_specs = (
        P(("groups", "member")),
        P(("groups", "member"), None, "fsdp"),
        P(("groups", "member"), None, "fsdp"),
        P(("groups", "member"), "fsdp", None),
        P(("groups", "member"), "fsdp"),
        P(("groups", "member"), "fsdp"),
        P(("groups", "member"), "fsdp"),
        P(("groups", "fsdp"), None, None),
    )
    return jax.shard_map(body, mesh=mesh, in_specs=in_specs, out_specs=out_specs, check_vma=False)
```

```python
import jax
import jax.numpy as jnp
import numpy as np
from jax import lax
from jax.experimental import pallas as pl
from jax.experimental.pallas import tpu as pltpu
from jax.sharding import PartitionSpec as P

eps = 1e-05
loss_scale = 256.0
f32 = jnp.float32
bf16 = jnp.bfloat16


def pair_terms(scores, pair_rows, entries, block_len):
    reward = jnp.mean(scores.reshape(entries, block_len), axis=1)
    slots = jnp.arange(entries, dtype=jnp.int32)
    select = (pair_rows[:, 0:1] == slots[None, :]).astype(f32) - (
        pair_rows[:, 1:2] == slots[None, :]
    ).astype(f32)
    margin = jnp.sum(select * reward[None, :], axis=1)
    total_loss = jnp.sum(jax.nn.softplus(-margin))
    weights = -jax.nn.sigmoid(-margin) * loss_scale
    dreward = jnp.sum(select * weights[:, None], axis=0)
    dscore = jnp.broadcast_to((dreward / block_len)[:, None], (entries, block_len)).reshape(-1)
    return (total_loss, dscore)


def contract(left, right, left_dim, right_dim):
    return lax.dot_general(
        left, right, (((left_dim,), (right_dim,)), ((), ())), preferred_element_type=f32
    )


class Ring:
    def __init__(self, nodes, position):
        order = list(range(0, nodes, 2)) + list(range(nodes - 1, 0, -2))
        self.nodes = nodes
        self.half = nodes // 2
        self.ahead = [(order[i], order[(i + 1) % nodes]) for i in range(nodes)]
        self.back = [(b, a) for a, b in self.ahead]
        place = {device: i for i, device in enumerate(order)}
        table = np.array(
            [[order[(place[d] + k) % nodes] for k in range(nodes)] for d in range(nodes)], np.int32
        )
        self.table = table
        row = lax.dynamic_index_in_dim(jnp.asarray(table), position, 0, keepdims=False)
        self.row = row
        self.device = [row[k] for k in range(nodes)]

    def visited(self, offsets, position):
        return lax.dynamic_index_in_dim(
            jnp.asarray(self.table[:, offsets]), position, 0, keepdims=False
        )

    def up(self, value):
        return lax.ppermute(value, "fsdp", self.ahead)

    def down(self, value):
        return lax.ppermute(value, "fsdp", self.back)

    def gather(self, own, visit):
        from_back = from_ahead = own
        middle = own.shape[0] // 2
        pending = [(0, own)]
        for step in range(1, self.half + 1):
            if step < self.half:
                from_back = self.up(from_back)
                from_ahead = self.down(from_ahead)
                arrived = [(self.nodes - step, from_back), (step, from_ahead)]
            else:
                first = self.up(from_back[:middle])
                second = self.down(from_ahead[middle:])
                arrived = [(step, jnp.concatenate([first, second], axis=0))]
            for offset, band in pending:
                visit(self.device[offset], band)
            pending = arrived
        for offset, band in pending:
            visit(self.device[offset], band)

    def scatter(self, part):
        far = part(self.device[self.half]).astype(bf16)
        middle = far.shape[0] // 2
        first = self.up(far[:middle])
        second = self.down(far[middle:])
        near_up = part(self.device[self.half - 1])
        near_down = part(self.device[self.half + 1])
        going_up = jnp.concatenate(
            [near_up[:middle] + first.astype(f32), near_up[middle:]], axis=0
        ).astype(bf16)
        going_down = jnp.concatenate(
            [near_down[:middle], near_down[middle:] + second.astype(f32)], axis=0
        ).astype(bf16)
        for step in range(self.half - 2, -1, -1):
            going_up = self.up(going_up)
            going_down = self.down(going_down)
            if step:
                going_up = (part(self.device[step]) + going_up.astype(f32)).astype(bf16)
                going_down = (
                    part(self.device[self.nodes - step]) + going_down.astype(f32)
                ).astype(bf16)
        own = part(self.device[0])
        return own + (going_up.astype(f32) + going_down.astype(f32))


def three_terms(value):
    high = lax.reduce_precision(value, 8, 7)
    rest = value - high
    middle = lax.reduce_precision(rest, 8, 7)
    return [term.astype(bf16) for term in (high, middle, rest - middle)]


def to_bands(value, nodes):
    return value.reshape(value.shape[:-1] + (nodes, value.shape[-1] // nodes))


def plain_body(features, blocks, pair_labels, ffn_gain, final_gain, score_head, w_gate, w_up, w_down):
    nodes = lax.axis_size("fsdp")
    position = lax.axis_index("fsdp")
    member = lax.axis_index("member")
    swap = [(0, 1), (1, 0)]
    ring = Ring(nodes, position)
    owned, block_len, width = features.shape
    columns = width // nodes
    half_rows = block_len // 2
    half_columns = columns // 2
    ids = blocks[0]
    entries = ids.shape[0]
    rows = entries * block_len
    w_gate = w_gate[0]
    w_up = w_up[0]
    w_down = w_down[0]
    hidden_count = w_gate.shape[1]
    w_gate_bands = w_gate.reshape(nodes, columns, hidden_count)
    w_up_bands = w_up.reshape(nodes, columns, hidden_count)

    def share(vector, device):
        return lax.dynamic_slice_in_dim(vector, device * columns, columns, 0)

    def down_band(device):
        return lax.dynamic_slice_in_dim(w_down, device * columns, columns, 1)

    other_ids = lax.ppermute(ids, "member", swap)
    sent_rows = lax.dynamic_slice_in_dim(features, member * half_rows, half_rows, 1)
    outgoing = jnp.transpose(to_bands(sent_rows, nodes), (2, 0, 1, 3))
    arrived = lax.all_to_all(outgoing, "fsdp", split_axis=0, concat_axis=0, tiled=True)
    near_half = arrived.reshape(nodes * owned, half_rows, columns)
    far_half = lax.ppermute(near_half, "member", swap)
    picked = jnp.zeros((entries, 2, half_rows, columns), bf16)
    picked = lax.dynamic_update_slice_in_dim(
        picked, jnp.take(near_half, ids, axis=0)[:, None], member, 1
    )
    picked = lax.dynamic_update_slice_in_dim(
        picked, jnp.take(far_half, ids, axis=0)[:, None], 1 - member, 1
    )
    band = picked.reshape(rows, columns)

    stored = features.astype(f32)
    inverse_own = lax.rsqrt(jnp.mean(stored * stored, axis=2) + eps)
    inverse_all = lax.all_gather(inverse_own, "fsdp", axis=0, tiled=True)
    inverse_in = jnp.take(inverse_all, ids, axis=0).reshape(rows, 1)

    gain = ffn_gain[0]
    gain_head = final_gain[0] * score_head[0]
    head_parts = jnp.stack(three_terms(gain_head))
    head_down = jnp.sum(contract(head_parts, w_down, 1, 1), axis=0)

    state = {"gate": None, "up": None, "scaled": jnp.zeros((nodes, rows, columns), bf16)}

    def add(total, value):
        return value if total is None else total + value

    def forward(device, arrived_band):
        scaled = (
            arrived_band.astype(f32) * inverse_in * share(gain, device)[None, :]
        ).astype(bf16)
        gate_band = lax.dynamic_index_in_dim(w_gate_bands, device, 0, keepdims=False)
        up_band = lax.dynamic_index_in_dim(w_up_bands, device, 0, keepdims=False)
        state["gate"] = add(state["gate"], contract(scaled, gate_band, 1, 0))
        state["up"] = add(state["up"], contract(scaled, up_band, 1, 0))
        state["scaled"] = lax.dynamic_update_index_in_dim(state["scaled"], scaled, device, 0)

    ring.gather(band, forward)
    gate_pre = state["gate"]
    up_pre = state["up"]
    sigmoid_gate = jax.nn.sigmoid(gate_pre)
    silu_gate = gate_pre * sigmoid_gate
    hidden = (silu_gate * up_pre).astype(bf16)
    inputs_band = band.astype(f32)
    score_part = jnp.sum(hidden.astype(f32) * head_down[None, :], axis=1) + jnp.sum(
        inputs_band * share(gain_head, position)[None, :], axis=1
    )
    score_parts = lax.all_gather(
        score_part.reshape(1, entries, block_len), "fsdp", axis=0, tiled=True
    )

    out_band = ring.scatter(lambda device: contract(hidden, down_band(device), 1, 0))
    summed_band = inputs_band + out_band

    state2 = {"back": None, "square": None, "summed": jnp.zeros((nodes, rows, columns), bf16)}

    def backward(device, arrived_band):
        wide = arrived_band.astype(f32)
        state2["back"] = add(state2["back"], contract(arrived_band, down_band(device), 1, 1))
        state2["square"] = add(state2["square"], jnp.sum(wide * wide, axis=1))
        state2["summed"] = lax.dynamic_update_index_in_dim(
            state2["summed"], arrived_band, device, 0
        )

    ring.gather(summed_band.astype(bf16), backward)
    inverse_out = lax.rsqrt(state2["square"] / width + eps)
    scores = inverse_out * jnp.sum(score_parts, axis=0).reshape(rows)
    total_loss, dscore = pair_terms(scores, pair_labels[0], entries, block_len)
    head_scale = inverse_out * dscore
    summed_scale = inverse_out * inverse_out * dscore * scores / width
    dhidden = head_scale[:, None] * head_down[None, :] - summed_scale[:, None] * state2["back"]
    grad_gate_pre = (
        dhidden * up_pre * sigmoid_gate * (1.0 + gate_pre * (1.0 - sigmoid_gate))
    ).astype(bf16)
    grad_up_pre = (dhidden * silu_gate).astype(bf16)
    inner_part = jnp.sum(
        grad_gate_pre.astype(f32) * gate_pre + grad_up_pre.astype(f32) * up_pre, axis=1
    )
    inner_parts = lax.all_gather(
        inner_part.reshape(1, entries, block_len), "fsdp", axis=0, tiled=True
    )

    def scaled_part(device):
        gate_band = lax.dynamic_index_in_dim(w_gate_bands, device, 0, keepdims=False)
        up_band = lax.dynamic_index_in_dim(w_up_bands, device, 0, keepdims=False)
        return contract(grad_gate_pre, gate_band, 1, 1) + contract(grad_up_pre, up_band, 1, 1)

    dscaled_band = ring.scatter(scaled_part)

    scaled_in = jnp.transpose(state["scaled"], (1, 0, 2)).reshape(rows, width)
    summed = jnp.transpose(state2["summed"], (1, 0, 2)).reshape(rows, width)
    dsummed_b = (
        head_scale[:, None] * gain_head[None, :] - summed_scale[:, None] * summed.astype(f32)
    ).astype(bf16)
    grad_gate = contract(scaled_in, grad_gate_pre, 0, 0).astype(bf16)
    grad_up = contract(scaled_in, grad_up_pre, 0, 0).astype(bf16)
    grad_down = contract(hidden, dsummed_b, 0, 0).astype(bf16)

    weighted = jnp.sum(head_scale[:, None] * summed_band, axis=0)
    grad_head = share(final_gain[0], position) * weighted
    grad_final = share(score_head[0], position) * weighted
    dsummed_band = (
        head_scale[:, None] * share(gain_head, position)[None, :]
        - summed_scale[:, None] * summed_band
    )

    normed_in_band = inputs_band * inverse_in
    grad_ffn = jnp.sum(dscaled_band * normed_in_band, axis=0)
    row_inner = jnp.sum(inner_parts, axis=0).reshape(rows, 1)
    drows = (
        inverse_in
        * (dscaled_band * share(gain, position)[None, :] - normed_in_band * (row_inner / width))
        + dsummed_band
    ).astype(bf16)

    kept = lax.dynamic_slice_in_dim(drows, member * half_columns, half_columns, 1)
    given = lax.dynamic_slice_in_dim(drows, (1 - member) * half_columns, half_columns, 1)
    taken = lax.ppermute(given, "member", swap)

    def by_block(listed, value):
        hit = listed[None, :] == jnp.arange(nodes * owned, dtype=jnp.int32)[:, None]
        value = value.reshape(entries, block_len, half_columns).astype(f32)
        total = sum(
            jnp.where(hit[:, entry, None, None], value[entry][None], 0.0)
            for entry in range(entries)
        )
        return total.astype(bf16).astype(f32)

    returned = (by_block(ids, kept) + by_block(other_ids, taken)).astype(bf16)
    returned = returned.reshape(nodes, owned, block_len, half_columns)
    mine = lax.all_to_all(returned, "fsdp", split_axis=0, concat_axis=0, tiled=True)
    other = lax.ppermute(mine, "member", swap)
    whole = jnp.zeros((2, nodes, owned, block_len, half_columns), bf16)
    whole = lax.dynamic_update_index_in_dim(whole, mine, member, 0)
    whole = lax.dynamic_update_index_in_dim(whole, other, 1 - member, 0)
    grad_features = jnp.transpose(whole, (2, 3, 1, 0, 4)).reshape(owned, block_len, width)
    return (
        total_loss.reshape(1),
        grad_gate[None],
        grad_up[None],
        grad_down[None],
        grad_head[None],
        grad_final[None],
        grad_ffn[None],
        grad_features,
    )


AUX = 16
STRIPE = 32
IN_SMEM = pl.BlockSpec(memory_space=pltpu.SMEM)
IN_VMEM = pl.BlockSpec(memory_space=pltpu.VMEM)
IN_HBM = pl.BlockSpec(memory_space=pltpu.HBM)


def dot(left, right, left_dim, right_dim):
    return contract(left, right, left_dim, right_dim)


def call(kernel, operands, specs, outs, scratch=(), limit=8, aliases=None, out_specs=None):
    operands = [
        pltpu.with_memory_space_constraint(value, pltpu.HBM) if spec is IN_HBM else value
        for value, spec in zip(operands, specs)
    ]
    return pl.pallas_call(
        kernel,
        out_shape=[jax.ShapeDtypeStruct(shape, dtype) for shape, dtype in outs],
        in_specs=specs,
        out_specs=out_specs or [IN_VMEM] * len(outs),
        scratch_shapes=list(scratch),
        input_output_aliases=aliases or {},
        compiler_params=pltpu.CompilerParams(vmem_limit_bytes=limit << 20),
    )(*operands)


def band_number(row_ref, offsets, k):
    if len(offsets) == 1:
        return row_ref[offsets[0]]
    return row_ref[offsets[0] + k * (offsets[1] - offsets[0])]


def stream(count, sources, weights, done, use):
    ways = len(sources)

    def copy(k, w):
        slot = k * ways + w
        return pltpu.make_async_copy(sources[w](k), weights.at[slot], done.at[slot])

    for k in range(count):
        for w in range(ways):
            copy(k, w).start()

    def step(k):
        for w in range(ways):
            copy(k, w).wait()
            use(k, w, weights.at[k * ways + w])

    if count == 1:
        return lambda: step(0)

    def run():
        def body(k, _):
            step(k)
            return 0

        lax.fori_loop(0, count, body, 0)

    return run


def rows_as_lanes(vectors):
    rows = vectors[0].shape[0]
    lane = lax.broadcasted_iota(jnp.int32, (rows, 128), 1)
    packed = jnp.zeros((rows, 128), f32)
    for k, vector in enumerate(vectors):
        packed = jnp.where(lane == k, vector, packed)
    return packed.T[:8]


def lanes_as_columns(vectors):
    rows = vectors[0].shape[1]
    line = lax.broadcasted_iota(jnp.int32, (128, rows), 0)
    packed = jnp.zeros((128, rows), f32)
    for k, vector in enumerate(vectors):
        packed = jnp.where(line == k, vector, packed)
    return packed.T


def split_terms(lanes):
    high = lanes.astype(bf16).astype(f32)
    rest = lanes - high
    middle = rest.astype(bf16).astype(f32)
    low = rest - middle
    top = jnp.concatenate([high, middle], axis=1)
    bottom = jnp.concatenate([low, jnp.zeros_like(low)], axis=1)
    return jnp.concatenate([top, bottom], axis=0).astype(bf16)


def joined_term(terms, k):
    half = terms.shape[1] // 2
    return terms[k : k + 1, :half] + terms[k : k + 1, half:] + terms[8 + k : 9 + k, :half]


def pieces_of(band):
    return band if isinstance(band, tuple) else (band,)


def pack_blocks(member, block, nodes):
    block_len, width = block.shape
    columns = width // nodes
    half = columns // 2

    def kernel(member_ref, block_ref, out):
        square = jnp.zeros((block_len, 1), f32)
        for d in range(nodes):
            part = block_ref[:, d * columns : (d + 1) * columns].astype(f32)
            square += jnp.sum(part * part, axis=1, keepdims=True)
        terms = split_terms(rows_as_lanes([lax.rsqrt(square / width + eps)]))
        for d in range(nodes):
            start = pl.multiple_of(d * columns + member_ref[0] * half, half)
            out[d, :block_len] = block_ref[:, pl.ds(start, half)]
            out[d, block_len:] = terms

    return call(
        kernel, [member, block], [IN_SMEM, IN_VMEM], [((nodes, block_len + AUX, half), bf16)]
    )[0]


def pick_blocks(ids, member, near, far):
    entries = ids.shape[0]
    block_len = near.shape[1] - AUX
    half = near.shape[2]

    def kernel(ids_ref, member_ref, near_ref, far_ref, band_out, inverse_out):
        first = member_ref[0] == 0
        for e in range(entries):
            mine, other = near_ref[ids_ref[e]], far_ref[ids_ref[e]]
            part = slice(e * block_len, (e + 1) * block_len)
            band_out[part, :half] = jnp.where(first, mine, other)[:block_len]
            band_out[part, half:] = jnp.where(first, other, mine)[:block_len]
            row = joined_term(mine[block_len:].astype(f32), 0)
            inverse_out[part] = lanes_as_columns([row])[:, 0:1]

    return call(
        kernel, [ids, member, near, far], [IN_SMEM, IN_SMEM, IN_VMEM, IN_VMEM],
        [((entries * block_len, 2 * half), bf16), ((entries * block_len, 1), f32)],
    )


def split_halves(back, ahead, middle):
    def kernel(back_ref, ahead_ref, first, second):
        first[...] = back_ref[:middle]
        second[...] = ahead_ref[middle:]

    columns = back.shape[1]
    return call(
        kernel, [back, ahead], [IN_VMEM] * 2,
        [((middle, columns), bf16), ((ahead.shape[0] - middle, columns), bf16)],
    )


def forward_bands(bands, row, offsets, gain_bands, inverse, gate_bands, up_bands, totals, final):
    bands = [pieces_of(band) for band in bands]
    flat = [piece for band in bands for piece in band]
    count = len(bands)
    rows, columns = inverse.shape[0], flat[0].shape[1]
    width = gate_bands.shape[2]
    last = final is not None
    far_offset = row.shape[0] // 2

    def kernel(row_ref, *refs):
        refs = list(refs)
        take = lambda k: [refs.pop(0) for _ in range(k)]
        band_refs = [take(len(band)) for band in bands]
        gain_ref, inverse_ref, gate_hbm, up_hbm = take(4)
        if totals:
            take(2)
        head_ref, down_hbm = take(2) if last else (None, None)
        totals_out = take(2)
        (scaled_out,) = take(1)
        if last:
            hidden_out, score_out, far_up, far_down = take(4)
        weights, done = take(2)

        def use(k, w, block):
            totals_out[w][...] += dot(scaled_out[k], block[...], 1, 0)

        run = stream(
            count,
            [
                lambda k: gate_hbm.at[band_number(row_ref, offsets, k)],
                lambda k: up_hbm.at[band_number(row_ref, offsets, k)],
            ],
            weights, done, use,
        )
        if last:
            far_weights, far_done = refs
            start = pl.multiple_of(row_ref[far_offset] * columns, columns)
            far_copy = pltpu.make_async_copy(
                down_hbm.at[:, pl.ds(start, columns)], far_weights, far_done
            )
            far_copy.start()
        for k in range(count):
            start = 0
            for ref in band_refs[k]:
                part = slice(start, start + ref.shape[0])
                scaled_out[k, part] = (
                    ref[...].astype(f32) * inverse_ref[part] * gain_ref[row_ref[offsets[k]]]
                ).astype(bf16)
                start += ref.shape[0]
        if not totals:
            for out in totals_out:
                out[...] = jnp.zeros_like(out)
        run()
        if last:
            gate_out, up_out = totals_out

            def finish(i, _):
                part = pl.ds(i * STRIPE, STRIPE)
                gate = gate_out[part]
                hidden = (gate * jax.nn.sigmoid(gate) * up_out[part]).astype(bf16)
                hidden_out[part] = hidden
                score_out[part] = jnp.sum(
                    hidden.astype(f32) * head_ref[...], axis=1, keepdims=True
                )
                return 0

            lax.fori_loop(0, rows // STRIPE, finish, 0)
            far_copy.wait()
            far = dot(hidden_out[...], far_weights[...], 1, 0).astype(bf16)
            far_up[...] = far[: rows // 2]
            far_down[...] = far[rows // 2 :]

    operands = [row] + flat + [gain_bands, inverse, gate_bands, up_bands]
    specs = [IN_SMEM] + [IN_VMEM] * (len(flat) + 2) + [IN_HBM, IN_HBM]
    aliases = {}
    if totals:
        aliases = {len(operands): 0, len(operands) + 1: 1}
        operands += list(totals)
        specs += [IN_VMEM] * 2
    outs = [((rows, width), f32)] * 2 + [((count, rows, columns), bf16)]
    scratch = [
        pltpu.VMEM((2 * count, columns, width), bf16), pltpu.SemaphoreType.DMA((2 * count,))
    ]
    if last:
        operands += list(final)
        specs += [IN_VMEM, IN_HBM]
        outs += [((rows, width), bf16), ((rows, 1), f32)] + [((rows // 2, columns), bf16)] * 2
        scratch += [pltpu.VMEM((width, columns), bf16), pltpu.SemaphoreType.DMA]
    out = call(kernel, operands, specs, outs, scratch, 8 + 4 * count, aliases)
    return out[:2], out[2], out[3:]


def pair_scales(notes, labels_ref, rows, entries, width):
    square, score = joined_term(notes, 0), joined_term(notes, 1)
    inverse_out = lax.rsqrt(square / width + eps)
    scores = inverse_out * score
    block_len = rows // entries
    rewards = [
        jnp.sum(scores[:, e * block_len : (e + 1) * block_len], axis=1, keepdims=True) / block_len
        for e in range(entries)
    ]
    drewards = [jnp.zeros((1, 1), f32) for _ in range(entries)]
    loss = jnp.zeros((1, 1), f32)
    for p in range(labels_ref.shape[0]):
        select = [
            (labels_ref[p, 0] == e).astype(f32) - (labels_ref[p, 1] == e).astype(f32)
            for e in range(entries)
        ]
        margin = sum(select[e] * rewards[e] for e in range(entries))
        loss += jnp.maximum(-margin, 0.0) + jnp.log1p(jnp.exp(-jnp.abs(margin)))
        weight = -jax.nn.sigmoid(-margin) * loss_scale
        drewards = [drewards[e] + select[e] * weight for e in range(entries)]
    lane = lax.broadcasted_iota(jnp.int32, (1, rows), 1)
    dscore = jnp.zeros((1, rows), f32)
    for e in range(entries):
        dscore = jnp.where(lane // block_len == e, drewards[e] / block_len, dscore)
    head_scale = inverse_out * dscore
    columns = lanes_as_columns([head_scale, inverse_out * head_scale * scores / width])
    return loss, columns[:, 0:1], columns[:, 1:2]


def backward_bands(bands, row, offsets, w_down, rows, total, final):
    bands = [pieces_of(band) for band in bands]
    flat = [piece for band in bands for piece in band]
    count = len(bands)
    columns = flat[0].shape[1]
    width, model_width = w_down.shape
    others = final[6] if final else []
    far_offset = row.shape[0] // 2

    def kernel(row_ref, *refs):
        refs = list(refs)
        take = lambda k: [refs.pop(0) for _ in range(k)]
        band_refs = [take(len(band)) for band in bands]
        (down_hbm,) = take(1)
        if total is not None:
            take(1)
        if final:
            gate_ref, up_ref, head_ref, labels_ref, gate_hbm, up_hbm = take(6)
            other_refs = take(len(others))
        (back_ref,) = take(1)
        if final:
            grads_out, inner_out, loss_out, head_scale, summed_scale, far_up, far_down = take(7)
        weights, done, kept = take(3)

        def use(k, w, block):
            back_ref[...] += dot(kept[k], block[...], 1, 1)

        def source(k):
            start = pl.multiple_of(band_number(row_ref, offsets, k) * columns, columns)
            return down_hbm.at[:, pl.ds(start, columns)]

        run = stream(count, [source], weights, done, use)
        if final:
            inner, far_weights, far_done = refs
            far_copies = [
                pltpu.make_async_copy(
                    source.at[row_ref[far_offset]], far_weights.at[w], far_done.at[w]
                )
                for w, source in enumerate((gate_hbm, up_hbm))
            ]
            for one in far_copies:
                one.start()
        for k in range(count):
            start = 0
            for ref in band_refs[k]:
                size = min(ref.shape[0], rows - start)
                kept[k, start : start + size] = ref[:size]
                start += size
        if total is None:
            back_ref[...] = jnp.zeros_like(back_ref)
        if final:
            tail = band_refs[-1][-1]
            notes = tail[tail.shape[0] - AUX :].astype(f32)
            for ref in other_refs:
                notes += ref[rows:].astype(f32)
            loss, head_column, summed_column = pair_scales(
                notes, labels_ref, rows, final[7], model_width
            )
            loss_out[...] = loss
            head_scale[...] = head_column
            summed_scale[...] = summed_column
        run()
        if not final:
            return

        def finish(i, _):
            part = pl.ds(i * STRIPE, STRIPE)
            gate, up = gate_ref[part], up_ref[part]
            sigmoid = jax.nn.sigmoid(gate)
            dhidden = head_scale[part] * head_ref[...] - summed_scale[part] * back_ref[part]
            dgate = (dhidden * up * sigmoid * (1.0 + gate * (1.0 - sigmoid))).astype(bf16)
            dup = (dhidden * (gate * sigmoid)).astype(bf16)
            grads_out[0, part] = dgate
            grads_out[1, part] = dup
            inner[part] = jnp.sum(
                dgate.astype(f32) * gate + dup.astype(f32) * up, axis=1, keepdims=True
            )
            return 0

        lax.fori_loop(0, rows // STRIPE, finish, 0)
        lanes = rows_as_lanes([inner[...]])
        inner_out[...] = lanes
        far_copies[0].wait()
        far = dot(grads_out[0], far_weights[0], 1, 1)
        far_copies[1].wait()
        far += dot(grads_out[1], far_weights[1], 1, 1)
        middle = rows // 2
        far_up[:middle] = far[:middle].astype(bf16)
        far_down[...] = far[middle:].astype(bf16)
        pad = jnp.zeros((AUX - 8, columns), f32)
        far_up[middle:] = jnp.concatenate([high_low(lanes), pad], axis=0).astype(bf16)

    operands = [row] + flat + [w_down]
    specs = [IN_SMEM] + [IN_VMEM] * len(flat) + [IN_HBM]
    aliases = {}
    if total is not None:
        aliases = {len(operands): 0}
        operands.append(total)
        specs.append(IN_VMEM)
    scratch = [
        pltpu.VMEM((count, width, columns), bf16), pltpu.SemaphoreType.DMA((count,)),
        pltpu.VMEM((count, rows, columns), bf16),
    ]
    outs = [((rows, width), f32)]
    if final:
        operands += list(final[:6]) + list(others)
        specs += [IN_VMEM] * 3 + [IN_SMEM] + [IN_HBM] * 2 + [IN_VMEM] * len(others)
        outs += [
            ((2, rows, width), bf16), ((8, rows), f32), ((1, 1), f32), ((rows, 1), f32),
            ((rows, 1), f32), ((rows // 2 + AUX, columns), bf16), ((rows // 2, columns), bf16),
        ]
        scratch += [
            pltpu.VMEM((rows, 1), f32), pltpu.VMEM((2, columns, width), bf16),
            pltpu.SemaphoreType.DMA((2,)),
        ]
    return call(kernel, operands, specs, outs, scratch, 10 + 3 * count, aliases)


def out_parts(row, offsets, hidden, w_down, columns):
    count = len(offsets)
    rows, width = hidden.shape

    def kernel(row_ref, hidden_ref, down_hbm, out, weights, done):
        def use(k, w, block):
            out[k] = dot(hidden_ref[...], block[...], 1, 0)

        def source(k):
            start = pl.multiple_of(band_number(row_ref, offsets, k) * columns, columns)
            return down_hbm.at[:, pl.ds(start, columns)]

        stream(count, [source], weights, done, use)()

    return call(
        kernel, [row, hidden, w_down], [IN_SMEM, IN_VMEM, IN_HBM],
        [((count, rows, columns), f32)],
        [pltpu.VMEM((count, width, columns), bf16), pltpu.SemaphoreType.DMA((count,))],
        4 + 3 * count,
    )[0]


def scaled_parts(row, offsets, grads, gate_bands, up_bands, down):
    count = len(offsets)
    rows, width = grads.shape[1:]
    columns = gate_bands.shape[1]
    order, first, bands, hidden_t, head_bands, head_scale, summed_scale, before = down
    flat = [piece for band in bands for piece in pieces_of(band)]
    extra = len(bands)
    nodes = gate_bands.shape[0]

    def kernel(row_ref, order_ref, grads_ref, gate_hbm, up_hbm, hidden_ref, head_ref,
               head_scale_ref, summed_scale_ref, *refs):
        band_refs = list(refs[: len(flat)])
        out, down_hbm, weights, done, made, sent, kept = refs[-7:]

        def use(k, w, block):
            term = dot(grads_ref[w], block[...], 1, 1)
            if w:
                out[k] += term
            else:
                out[k] = term

        run = stream(
            count,
            [
                lambda k: gate_hbm.at[band_number(row_ref, offsets, k)],
                lambda k: up_hbm.at[band_number(row_ref, offsets, k)],
            ],
            weights, done, use,
        )
        for j, band in enumerate(bands):
            start = 0
            for _ in pieces_of(band):
                ref = band_refs.pop(0)
                size = min(ref.shape[0], rows - start)
                kept[j, start : start + size] = ref[:size]
                start += size

        def leave(j):
            start = pl.multiple_of(order_ref[first + j] * columns, columns)
            return pltpu.make_async_copy(
                made.at[j], down_hbm.at[:, pl.ds(start, columns)], sent.at[j]
            )

        def make(j, _):
            dsummed = (
                head_scale_ref[...] * head_ref[order_ref[first + j]]
                - summed_scale_ref[...] * kept[j].astype(f32)
            )
            made[j] = dot(hidden_ref[...], dsummed.astype(bf16), 1, 0).astype(bf16)
            leave(j).start()
            return 0

        lax.fori_loop(0, extra, make, 0)
        run()
        for j in range(extra):
            leave(j).wait()

    operands = [row, order, grads, gate_bands, up_bands, hidden_t, head_bands, head_scale]
    operands += [summed_scale] + flat
    specs = [IN_SMEM, IN_SMEM, IN_VMEM, IN_HBM, IN_HBM] + [IN_VMEM] * (4 + len(flat))
    aliases = None
    if before is not None:
        aliases = {len(operands): 1}
        operands.append(before)
        specs.append(IN_HBM)
    return call(
        kernel, operands, specs,
        [((count, rows, columns), f32), ((width, nodes * columns), bf16)],
        [
            pltpu.VMEM((2 * count, columns, width), bf16),
            pltpu.SemaphoreType.DMA((2 * count,)),
            pltpu.VMEM((extra, width, columns), bf16), pltpu.SemaphoreType.DMA((extra,)),
            pltpu.VMEM((extra, rows, columns), bf16),
        ],
        6 + 4 * count + 3 * extra, aliases, [IN_VMEM, IN_HBM],
    )


def high_low(row):
    high = row.astype(bf16).astype(f32)
    return jnp.concatenate([high, row - high], axis=1)


def add_arrivals(parts, from_back, from_ahead, inner):
    rows, columns = parts.shape[1:]
    middle = rows // 2
    tail = 0 if inner is None else AUX
    early = from_back.shape[0] < rows

    def kernel(*refs):
        parts_ref, back_ref, ahead_ref = refs[:3]
        out_up, out_down = refs[-2:]
        if early:
            out_up[:middle] = (parts_ref[0, :middle] + back_ref[:middle].astype(f32)).astype(bf16)
            out_up[middle:rows] = parts_ref[0, middle:].astype(bf16)
            out_down[:middle] = parts_ref[1, :middle].astype(bf16)
            out_down[middle:rows] = (
                parts_ref[1, middle:] + ahead_ref[:middle].astype(f32)
            ).astype(bf16)
        else:
            out_up[:rows] = (parts_ref[0] + back_ref[:rows].astype(f32)).astype(bf16)
            out_down[:rows] = (parts_ref[1] + ahead_ref[:rows].astype(f32)).astype(bf16)
        if tail:
            row = refs[3][...]
            base = middle if early else rows
            pad = jnp.zeros((AUX - 8, columns), f32)

            def carry(ref):
                came = ref[base:].astype(f32)[:8]
                return row + came[:, : columns // 2] + came[:, columns // 2 :]

            up_row = carry(back_ref)
            down_row = row if early else carry(ahead_ref)
            out_up[rows:] = jnp.concatenate([high_low(up_row), pad], axis=0).astype(bf16)
            out_down[rows:] = jnp.concatenate([high_low(down_row), pad], axis=0).astype(bf16)

    operands = [parts, from_back, from_ahead] + ([] if inner is None else [inner])
    return call(
        kernel, operands, [IN_VMEM] * len(operands), [((rows + tail, columns), bf16)] * 2
    )


def finish_summed(own, from_back, from_ahead, band, head_row, score):
    rows, columns = own.shape[1:]

    def kernel(own_ref, back_ref, ahead_ref, band_ref, head_ref, score_ref, summed_out, message):
        inputs = band_ref[...].astype(f32)
        summed = inputs + (
            own_ref[0] + (back_ref[...].astype(f32) + ahead_ref[...].astype(f32))
        )
        summed_out[...] = summed
        message[:rows] = summed.astype(bf16)
        square = jnp.sum(summed * summed, axis=1, keepdims=True)
        share = score_ref[...] + jnp.sum(inputs * head_ref[...], axis=1, keepdims=True)
        message[rows:] = split_terms(rows_as_lanes([square, share]))

    return call(
        kernel, [own, from_back, from_ahead, band, head_row, score], [IN_VMEM] * 6,
        [((rows, columns), f32), ((rows + AUX, columns), bf16)],
    )


def finish_rows(member, own, from_back, from_ahead, inner, band, summed, inverse, gain_row,
                head_row, head_scale, summed_scale, final_row, score_row, entries, width):
    rows, columns = own.shape[1:]
    block_len = rows // entries
    half = block_len // 2

    def kernel(member_ref, own_ref, back_ref, ahead_ref, inner_ref, band_ref, summed_ref,
               inverse_ref, gain_ref, head_ref, head_scale_ref, summed_scale_ref, final_ref,
               score_ref, kept_out, given_out, ffn_out, head_out, final_out, drows):
        dscaled = own_ref[0] + (back_ref[:rows].astype(f32) + ahead_ref[:rows].astype(f32))
        came = (back_ref[rows:].astype(f32) + ahead_ref[rows:].astype(f32))[:8]
        lanes = inner_ref[...] + came[:, : columns // 2] + came[:, columns // 2 :]
        inner_column = lanes_as_columns([lanes[0:1]])[:, 0:1]
        inverse_in = inverse_ref[...]
        normed = band_ref[...].astype(f32) * inverse_in
        ffn_out[...] = jnp.sum(dscaled * normed, axis=0, keepdims=True)
        summed = summed_ref[...]
        weighted = jnp.sum(head_scale_ref[...] * summed, axis=0, keepdims=True)
        head_out[...] = final_ref[...] * weighted
        final_out[...] = score_ref[...] * weighted
        dsummed = head_scale_ref[...] * head_ref[...] - summed_scale_ref[...] * summed
        drows[...] = (
            inverse_in * (dscaled * gain_ref[...] - normed * (inner_column / width)) + dsummed
        ).astype(bf16)
        for e in range(entries):
            for out, which in ((kept_out, member_ref[0]), (given_out, 1 - member_ref[0])):
                start = pl.multiple_of(e * block_len + which * half, half)
                out[e] = drows[pl.ds(start, half)]

    return call(
        kernel,
        [member, own, from_back, from_ahead, inner, band, summed, inverse, gain_row, head_row,
         head_scale, summed_scale, final_row, score_row],
        [IN_SMEM] + [IN_VMEM] * 13,
        [((entries, half, columns), bf16)] * 2 + [((1, columns), f32)] * 3,
        [pltpu.VMEM((rows, columns), bf16)],
    )


def route_rows(ids, other_ids, kept, taken, blocks):
    entries, half, columns = kept.shape

    def kernel(ids_ref, other_ref, kept_ref, taken_ref, out):
        def route(b, _):
            sums = []
            for listed, value in ((ids_ref, kept_ref), (other_ref, taken_ref)):
                total = sum(
                    jnp.where(listed[e] == b, value[e].astype(f32), 0.0) for e in range(entries)
                )
                sums.append(total.astype(bf16).astype(f32))
            out[b] = (sums[0] + sums[1]).astype(bf16)
            return 0

        lax.fori_loop(0, blocks, route, 0)

    return call(
        kernel, [ids, other_ids, kept, taken], [IN_SMEM, IN_SMEM, IN_VMEM, IN_VMEM],
        [((blocks, half, columns), bf16)],
    )[0]


def assemble_block(member, mine, other):
    nodes, half, columns = mine.shape

    def kernel(member_ref, mine_ref, other_ref, out):
        for value, which in ((mine_ref, member_ref[0]), (other_ref, 1 - member_ref[0])):
            part = pl.ds(pl.multiple_of(which * half, half), half)
            for d in range(nodes):
                out[part, d * columns : (d + 1) * columns] = value[d]

    return call(
        kernel, [member, mine, other], [IN_SMEM, IN_VMEM, IN_VMEM],
        [((2 * half, nodes * columns), bf16)],
    )[0]


def turned(value):
    def kernel(value_ref, out):
        out[...] = value_ref[...].T

    return call(kernel, [value], [IN_VMEM], [(value.shape[::-1], value.dtype)])[0]


def whole(*shape):
    zeros = (0,) * len(shape)
    return pl.BlockSpec(shape, lambda *_: zeros)


def grid_call(kernel, index, operands, specs, outs, out_specs, steps, scratch, aliases=None):
    return pl.pallas_call(
        kernel,
        out_shape=[jax.ShapeDtypeStruct(shape, dtype) for shape, dtype in outs],
        grid_spec=pltpu.PrefetchScalarGridSpec(
            num_scalar_prefetch=1, grid=(steps,), in_specs=specs, out_specs=out_specs,
            scratch_shapes=list(scratch),
        ),
        input_output_aliases=aliases or {},
        compiler_params=pltpu.CompilerParams(vmem_limit_bytes=20 << 20),
    )(index, *operands)


def weight_grads(index, stacks, grads):
    nodes = sum(stack.shape[0] for stack in stacks)
    _, rows, columns = stacks[0].shape
    width = grads.shape[2]

    def kernel(index_ref, *refs):
        grads_ref, gate_out, up_out, kept, done = refs[len(stacks) :]

        @pl.when(pl.program_id(0) == 0)
        def _():
            copies = []
            start = 0
            for n, ref in enumerate(refs[: len(stacks)]):
                copies.append(
                    pltpu.make_async_copy(
                        ref, kept.at[pl.ds(start, ref.shape[0])], done.at[n]
                    )
                )
                copies[-1].start()
                start += ref.shape[0]
            for one in copies:
                one.wait()

        scaled = kept[pl.program_id(0)].T
        gate_out[0] = dot(scaled, grads_ref[0], 1, 0).astype(bf16)
        up_out[0] = dot(scaled, grads_ref[1], 1, 0).astype(bf16)

    out = pl.BlockSpec((1, columns, width), lambda b, idx: (idx[b], 0, 0))
    stacks = [pltpu.with_memory_space_constraint(stack, pltpu.HBM) for stack in stacks]
    return grid_call(
        kernel, index, stacks + [grads], [IN_HBM] * len(stacks) + [IN_VMEM],
        [((nodes, columns, width), bf16)] * 2, [out, out], nodes,
        [
            pltpu.VMEM((nodes, rows, columns), bf16),
            pltpu.SemaphoreType.DMA((len(stacks),)),
        ],
    )


def after(values, *others):
    return lax.optimization_barrier(tuple(values) + tuple(others))[: len(values)]


def ring_body(features, blocks, pair_labels, ffn_gain, final_gain, score_head, w_gate, w_up, w_down):
    nodes = lax.axis_size("fsdp")
    position = lax.axis_index("fsdp")
    member = lax.axis_index("member").reshape(1)
    swap = [(0, 1), (1, 0)]
    ring = Ring(nodes, position)
    half = ring.half
    block_len, width = features.shape[1:]
    columns = width // nodes
    ids = blocks[0]
    entries = ids.shape[0]
    rows = entries * block_len
    middle = rows // 2
    w_gate = w_gate[0]
    w_up = w_up[0]
    w_down = w_down[0]
    hidden_count = w_gate.shape[1]
    gate_bands = w_gate.reshape(nodes, columns, hidden_count)
    up_bands = w_up.reshape(nodes, columns, hidden_count)
    gain_head = final_gain[0] * score_head[0]
    gain_bands = ffn_gain.reshape(nodes, 1, columns)
    head_bands = gain_head.reshape(nodes, 1, columns)

    def share(vector):
        return lax.dynamic_slice_in_dim(vector, position * columns, columns, 0)[None]

    other_ids = lax.ppermute(ids, "member", swap)
    sent = pack_blocks(member, features[0], nodes)
    near = lax.all_to_all(sent, "fsdp", split_axis=0, concat_axis=0, tiled=True)
    head_parts = jnp.stack(three_terms(gain_head))
    head_down = jnp.sum(contract(head_parts, w_down, 1, 1), axis=0)[None]
    near, other_ids = after([near, other_ids], head_down)
    far = lax.ppermute(near, "member", swap)
    band, inverse_in = pick_blocks(ids, member, near, far)

    def gather(own, visit, extra=None):
        back = ahead = own
        total = None
        pending, pending_offsets = [own], [0]
        order = []
        for step in range(1, half + 1):
            if step < half:
                back, ahead = ring.up(back), ring.down(ahead)
                arrived, offsets = [back, ahead], [nodes - step, step]
            else:
                first, second = split_halves(back, ahead, middle)
                arrived, offsets = [(ring.up(first), ring.down(second))], [step]
            total = visit(pending, pending_offsets, total)
            order += pending_offsets
            if step < half:
                done = list(total)
                if step == 1 and extra is not None:
                    done.append(extra)
                back, ahead = after([back, ahead], *done)
                arrived = [back, ahead]
            pending, pending_offsets = arrived, offsets
        order += pending_offsets
        return pending, pending_offsets, total, order

    scaled = []

    def forward(bands, offsets, total, final=None):
        total, new, rest = forward_bands(
            bands, ring.row, offsets, gain_bands, inverse_in, gate_bands, up_bands, total, final
        )
        scaled.append(new)
        return total if final is None else (total, rest)

    last, last_offsets, total, offsets = gather(band, forward)
    order = ring.visited(offsets, position)
    (gate_pre, up_pre), (hidden, score, up_message, down_message) = forward(
        last, last_offsets, total, (head_down, w_down)
    )
    (held,) = after([hidden], up_message)
    back, ahead = ring.up(up_message), ring.down(down_message)
    for step in range(half - 1, 0, -1):
        parts = out_parts(ring.row, [step, nodes - step], held, w_down, columns)
        (held,) = after([held], back, ahead)
        back, ahead = add_arrivals(parts, back, ahead, None)
        back, ahead = ring.up(back), ring.down(ahead)
    own_part = out_parts(ring.row, [0], held, w_down, columns)
    summed_band, message = finish_summed(
        own_part, back, ahead, band, share(gain_head), score
    )

    messages = []

    def backward(bands, offsets, total, final=None):
        messages.extend(bands)
        return backward_bands(
            bands, ring.row, offsets, w_down, rows, None if total is None else total[0], final
        )

    (held,) = after([hidden], message)
    hidden_t = turned(held)
    last, last_offsets, total, _ = gather(message, backward, hidden_t)
    _, grads, inner, loss, head_scale, summed_scale, up_message, down_message = backward(
        last, last_offsets, total,
        (
            gate_pre, up_pre, head_down, pair_labels[0], gate_bands, up_bands, list(messages),
            entries,
        ),
    )

    (held,) = after([grads], up_message)
    back, ahead = ring.up(up_message), ring.down(down_message)
    bounds = [0, 1, 3, 5, nodes]

    def parts_and_down(offsets, held, piece, before):
        start, stop = bounds[piece], bounds[piece + 1]
        return scaled_parts(
            ring.row, offsets, held, gate_bands, up_bands,
            (
                order, start, messages[start:stop], hidden_t, head_bands, head_scale,
                summed_scale, before,
            ),
        )

    grad_down = None
    for step in range(half - 1, 0, -1):
        parts, grad_down = parts_and_down(
            [step, nodes - step], held, half - 1 - step, grad_down
        )
        (held,) = after([held], back, ahead)
        back, ahead = add_arrivals(parts, back, ahead, inner)
        back, ahead = ring.up(back), ring.down(ahead)
    own_part, grad_down = parts_and_down([0], held, half - 1, grad_down)
    kept, given, grad_ffn, grad_head, grad_final = finish_rows(
        member, own_part, back, ahead, inner, band, summed_band, inverse_in,
        share(ffn_gain[0]), share(gain_head), head_scale, summed_scale, share(final_gain[0]),
        share(score_head[0]), entries, width,
    )

    (held,) = after([grads], given)
    taken = lax.ppermute(given, "member", swap)
    returned = route_rows(ids, other_ids, kept, taken, nodes)
    mine = lax.all_to_all(returned, "fsdp", split_axis=0, concat_axis=0, tiled=True)
    grad_gate, grad_up = weight_grads(order, scaled, held)
    (mine,) = after([mine], grad_gate, grad_up)
    other = lax.ppermute(mine, "member", swap)
    grad_features = assemble_block(member, mine, other)
    return (
        loss.reshape(1),
        grad_gate.reshape(1, width, hidden_count),
        grad_up.reshape(1, width, hidden_count),
        grad_down[None],
        grad_head,
        grad_final,
        grad_ffn,
        grad_features[None],
    )


def body(features, blocks, pair_labels, ffn_gain, final_gain, score_head, w_gate, w_up, w_down):
    nodes = lax.axis_size("fsdp")
    rows = blocks.shape[1] * features.shape[1]
    columns = features.shape[2] // nodes
    tiled = w_gate.shape[2] % 256 == 0 and columns == 2 * rows and rows % 256 == 0
    single = features.shape[0] == 1 and lax.axis_size("member") == 2
    chosen = ring_body if tiled and single and nodes == 8 else plain_body
    return chosen(
        features, blocks, pair_labels, ffn_gain, final_gain, score_head, w_gate, w_up, w_down
    )


def solution(mesh):
    in_specs = (
        P(("groups", "fsdp"), None, None),
        P(("groups", "member"), None),
        P(("groups", "member"), None, None),
        P("member", None),
        P("member", None),
        P("member", None),
        P("member", None, "fsdp"),
        P("member", None, "fsdp"),
        P("member", "fsdp", None),
    )
    out_specs = (
        P(("groups", "member")),
        P(("groups", "member"), None, "fsdp"),
        P(("groups", "member"), None, "fsdp"),
        P(("groups", "member"), "fsdp", None),
        P(("groups", "member"), "fsdp"),
        P(("groups", "member"), "fsdp"),
        P(("groups", "member"), "fsdp"),
        P(("groups", "fsdp"), None, None),
    )
    return jax.shard_map(body, mesh=mesh, in_specs=in_specs, out_specs=out_specs, check_vma=False)
```

```python
import jax
import jax.numpy as jnp
import numpy as np
from jax import lax
from jax.experimental import pallas as pl
from jax.experimental.pallas import tpu as pltpu
from jax.sharding import PartitionSpec as P

eps = 1e-05
loss_scale = 256.0
f32 = jnp.float32
bf16 = jnp.bfloat16


def pair_terms(scores, pair_rows, entries, block_len):
    reward = jnp.mean(scores.reshape(entries, block_len), axis=1)
    slots = jnp.arange(entries, dtype=jnp.int32)
    select = (pair_rows[:, 0:1] == slots[None, :]).astype(f32) - (
        pair_rows[:, 1:2] == slots[None, :]
    ).astype(f32)
    margin = jnp.sum(select * reward[None, :], axis=1)
    total_loss = jnp.sum(jax.nn.softplus(-margin))
    weights = -jax.nn.sigmoid(-margin) * loss_scale
    dreward = jnp.sum(select * weights[:, None], axis=0)
    dscore = jnp.broadcast_to((dreward / block_len)[:, None], (entries, block_len)).reshape(-1)
    return (total_loss, dscore)


def contract(left, right, left_dim, right_dim):
    return lax.dot_general(
        left, right, (((left_dim,), (right_dim,)), ((), ())), preferred_element_type=f32
    )


class Ring:
    def __init__(self, nodes, position):
        order = list(range(0, nodes, 2)) + list(range(nodes - 1, 0, -2))
        self.nodes = nodes
        self.half = nodes // 2
        self.ahead = [(order[i], order[(i + 1) % nodes]) for i in range(nodes)]
        self.back = [(b, a) for a, b in self.ahead]
        place = {device: i for i, device in enumerate(order)}
        table = np.array(
            [[order[(place[d] + k) % nodes] for k in range(nodes)] for d in range(nodes)], np.int32
        )
        self.table = table
        row = lax.dynamic_index_in_dim(jnp.asarray(table), position, 0, keepdims=False)
        self.row = row
        self.device = [row[k] for k in range(nodes)]

    def visited(self, offsets, position):
        return lax.dynamic_index_in_dim(
            jnp.asarray(self.table[:, offsets]), position, 0, keepdims=False
        )

    def up(self, value):
        return lax.ppermute(value, "fsdp", self.ahead)

    def down(self, value):
        return lax.ppermute(value, "fsdp", self.back)

    def gather(self, own, visit):
        from_back = from_ahead = own
        middle = own.shape[0] // 2
        pending = [(0, own)]
        for step in range(1, self.half + 1):
            if step < self.half:
                from_back = self.up(from_back)
                from_ahead = self.down(from_ahead)
                arrived = [(self.nodes - step, from_back), (step, from_ahead)]
            else:
                first = self.up(from_back[:middle])
                second = self.down(from_ahead[middle:])
                arrived = [(step, jnp.concatenate([first, second], axis=0))]
            for offset, band in pending:
                visit(self.device[offset], band)
            pending = arrived
        for offset, band in pending:
            visit(self.device[offset], band)

    def scatter(self, part):
        far = part(self.device[self.half]).astype(bf16)
        middle = far.shape[0] // 2
        first = self.up(far[:middle])
        second = self.down(far[middle:])
        near_up = part(self.device[self.half - 1])
        near_down = part(self.device[self.half + 1])
        going_up = jnp.concatenate(
            [near_up[:middle] + first.astype(f32), near_up[middle:]], axis=0
        ).astype(bf16)
        going_down = jnp.concatenate(
            [near_down[:middle], near_down[middle:] + second.astype(f32)], axis=0
        ).astype(bf16)
        for step in range(self.half - 2, -1, -1):
            going_up = self.up(going_up)
            going_down = self.down(going_down)
            if step:
                going_up = (part(self.device[step]) + going_up.astype(f32)).astype(bf16)
                going_down = (
                    part(self.device[self.nodes - step]) + going_down.astype(f32)
                ).astype(bf16)
        own = part(self.device[0])
        return own + (going_up.astype(f32) + going_down.astype(f32))


def three_terms(value):
    high = lax.reduce_precision(value, 8, 7)
    rest = value - high
    middle = lax.reduce_precision(rest, 8, 7)
    return [term.astype(bf16) for term in (high, middle, rest - middle)]


def to_bands(value, nodes):
    return value.reshape(value.shape[:-1] + (nodes, value.shape[-1] // nodes))


def plain_body(features, blocks, pair_labels, ffn_gain, final_gain, score_head, w_gate, w_up, w_down):
    nodes = lax.axis_size("fsdp")
    position = lax.axis_index("fsdp")
    member = lax.axis_index("member")
    swap = [(0, 1), (1, 0)]
    ring = Ring(nodes, position)
    owned, block_len, width = features.shape
    columns = width // nodes
    half_rows = block_len // 2
    half_columns = columns // 2
    ids = blocks[0]
    entries = ids.shape[0]
    rows = entries * block_len
    w_gate = w_gate[0]
    w_up = w_up[0]
    w_down = w_down[0]
    hidden_count = w_gate.shape[1]
    w_gate_bands = w_gate.reshape(nodes, columns, hidden_count)
    w_up_bands = w_up.reshape(nodes, columns, hidden_count)

    def share(vector, device):
        return lax.dynamic_slice_in_dim(vector, device * columns, columns, 0)

    def down_band(device):
        return lax.dynamic_slice_in_dim(w_down, device * columns, columns, 1)

    other_ids = lax.ppermute(ids, "member", swap)
    sent_rows = lax.dynamic_slice_in_dim(features, member * half_rows, half_rows, 1)
    outgoing = jnp.transpose(to_bands(sent_rows, nodes), (2, 0, 1, 3))
    arrived = lax.all_to_all(outgoing, "fsdp", split_axis=0, concat_axis=0, tiled=True)
    near_half = arrived.reshape(nodes * owned, half_rows, columns)
    far_half = lax.ppermute(near_half, "member", swap)
    picked = jnp.zeros((entries, 2, half_rows, columns), bf16)
    picked = lax.dynamic_update_slice_in_dim(
        picked, jnp.take(near_half, ids, axis=0)[:, None], member, 1
    )
    picked = lax.dynamic_update_slice_in_dim(
        picked, jnp.take(far_half, ids, axis=0)[:, None], 1 - member, 1
    )
    band = picked.reshape(rows, columns)

    stored = features.astype(f32)
    inverse_own = lax.rsqrt(jnp.mean(stored * stored, axis=2) + eps)
    inverse_all = lax.all_gather(inverse_own, "fsdp", axis=0, tiled=True)
    inverse_in = jnp.take(inverse_all, ids, axis=0).reshape(rows, 1)

    gain = ffn_gain[0]
    gain_head = final_gain[0] * score_head[0]
    head_parts = jnp.stack(three_terms(gain_head))
    head_down = jnp.sum(contract(head_parts, w_down, 1, 1), axis=0)

    state = {"gate": None, "up": None, "scaled": jnp.zeros((nodes, rows, columns), bf16)}

    def add(total, value):
        return value if total is None else total + value

    def forward(device, arrived_band):
        scaled = (
            arrived_band.astype(f32) * inverse_in * share(gain, device)[None, :]
        ).astype(bf16)
        gate_band = lax.dynamic_index_in_dim(w_gate_bands, device, 0, keepdims=False)
        up_band = lax.dynamic_index_in_dim(w_up_bands, device, 0, keepdims=False)
        state["gate"] = add(state["gate"], contract(scaled, gate_band, 1, 0))
        state["up"] = add(state["up"], contract(scaled, up_band, 1, 0))
        state["scaled"] = lax.dynamic_update_index_in_dim(state["scaled"], scaled, device, 0)

    ring.gather(band, forward)
    gate_pre = state["gate"]
    up_pre = state["up"]
    sigmoid_gate = jax.nn.sigmoid(gate_pre)
    silu_gate = gate_pre * sigmoid_gate
    hidden = (silu_gate * up_pre).astype(bf16)
    inputs_band = band.astype(f32)
    score_part = jnp.sum(hidden.astype(f32) * head_down[None, :], axis=1) + jnp.sum(
        inputs_band * share(gain_head, position)[None, :], axis=1
    )
    score_parts = lax.all_gather(
        score_part.reshape(1, entries, block_len), "fsdp", axis=0, tiled=True
    )

    out_band = ring.scatter(lambda device: contract(hidden, down_band(device), 1, 0))
    summed_band = inputs_band + out_band

    state2 = {"back": None, "square": None, "summed": jnp.zeros((nodes, rows, columns), bf16)}

    def backward(device, arrived_band):
        wide = arrived_band.astype(f32)
        state2["back"] = add(state2["back"], contract(arrived_band, down_band(device), 1, 1))
        state2["square"] = add(state2["square"], jnp.sum(wide * wide, axis=1))
        state2["summed"] = lax.dynamic_update_index_in_dim(
            state2["summed"], arrived_band, device, 0
        )

    ring.gather(summed_band.astype(bf16), backward)
    inverse_out = lax.rsqrt(state2["square"] / width + eps)
    scores = inverse_out * jnp.sum(score_parts, axis=0).reshape(rows)
    total_loss, dscore = pair_terms(scores, pair_labels[0], entries, block_len)
    head_scale = inverse_out * dscore
    summed_scale = inverse_out * inverse_out * dscore * scores / width
    dhidden = head_scale[:, None] * head_down[None, :] - summed_scale[:, None] * state2["back"]
    grad_gate_pre = (
        dhidden * up_pre * sigmoid_gate * (1.0 + gate_pre * (1.0 - sigmoid_gate))
    ).astype(bf16)
    grad_up_pre = (dhidden * silu_gate).astype(bf16)
    inner_part = jnp.sum(
        grad_gate_pre.astype(f32) * gate_pre + grad_up_pre.astype(f32) * up_pre, axis=1
    )
    inner_parts = lax.all_gather(
        inner_part.reshape(1, entries, block_len), "fsdp", axis=0, tiled=True
    )

    def scaled_part(device):
        gate_band = lax.dynamic_index_in_dim(w_gate_bands, device, 0, keepdims=False)
        up_band = lax.dynamic_index_in_dim(w_up_bands, device, 0, keepdims=False)
        return contract(grad_gate_pre, gate_band, 1, 1) + contract(grad_up_pre, up_band, 1, 1)

    dscaled_band = ring.scatter(scaled_part)

    scaled_in = jnp.transpose(state["scaled"], (1, 0, 2)).reshape(rows, width)
    summed = jnp.transpose(state2["summed"], (1, 0, 2)).reshape(rows, width)
    dsummed_b = (
        head_scale[:, None] * gain_head[None, :] - summed_scale[:, None] * summed.astype(f32)
    ).astype(bf16)
    grad_gate = contract(scaled_in, grad_gate_pre, 0, 0).astype(bf16)
    grad_up = contract(scaled_in, grad_up_pre, 0, 0).astype(bf16)
    grad_down = contract(hidden, dsummed_b, 0, 0).astype(bf16)

    weighted = jnp.sum(head_scale[:, None] * summed_band, axis=0)
    grad_head = share(final_gain[0], position) * weighted
    grad_final = share(score_head[0], position) * weighted
    dsummed_band = (
        head_scale[:, None] * share(gain_head, position)[None, :]
        - summed_scale[:, None] * summed_band
    )

    normed_in_band = inputs_band * inverse_in
    grad_ffn = jnp.sum(dscaled_band * normed_in_band, axis=0)
    row_inner = jnp.sum(inner_parts, axis=0).reshape(rows, 1)
    drows = (
        inverse_in
        * (dscaled_band * share(gain, position)[None, :] - normed_in_band * (row_inner / width))
        + dsummed_band
    ).astype(bf16)

    kept = lax.dynamic_slice_in_dim(drows, member * half_columns, half_columns, 1)
    given = lax.dynamic_slice_in_dim(drows, (1 - member) * half_columns, half_columns, 1)
    taken = lax.ppermute(given, "member", swap)

    def by_block(listed, value):
        hit = listed[None, :] == jnp.arange(nodes * owned, dtype=jnp.int32)[:, None]
        value = value.reshape(entries, block_len, half_columns).astype(f32)
        total = sum(
            jnp.where(hit[:, entry, None, None], value[entry][None], 0.0)
            for entry in range(entries)
        )
        return total.astype(bf16).astype(f32)

    returned = (by_block(ids, kept) + by_block(other_ids, taken)).astype(bf16)
    returned = returned.reshape(nodes, owned, block_len, half_columns)
    mine = lax.all_to_all(returned, "fsdp", split_axis=0, concat_axis=0, tiled=True)
    other = lax.ppermute(mine, "member", swap)
    whole = jnp.zeros((2, nodes, owned, block_len, half_columns), bf16)
    whole = lax.dynamic_update_index_in_dim(whole, mine, member, 0)
    whole = lax.dynamic_update_index_in_dim(whole, other, 1 - member, 0)
    grad_features = jnp.transpose(whole, (2, 3, 1, 0, 4)).reshape(owned, block_len, width)
    return (
        total_loss.reshape(1),
        grad_gate[None],
        grad_up[None],
        grad_down[None],
        grad_head[None],
        grad_final[None],
        grad_ffn[None],
        grad_features,
    )


AUX = 16
STRIPE = 128
CHUNK = 256
IN_SMEM = pl.BlockSpec(memory_space=pltpu.SMEM)
IN_VMEM = pl.BlockSpec(memory_space=pltpu.VMEM)
IN_HBM = pl.BlockSpec(memory_space=pltpu.HBM)


def dot(left, right, left_dim, right_dim):
    return contract(left, right, left_dim, right_dim)


def call(kernel, operands, specs, outs, scratch=(), limit=8, aliases=None, out_specs=None):
    operands = [
        pltpu.with_memory_space_constraint(value, pltpu.HBM) if spec is IN_HBM else value
        for value, spec in zip(operands, specs)
    ]
    return pl.pallas_call(
        kernel,
        out_shape=[jax.ShapeDtypeStruct(shape, dtype) for shape, dtype in outs],
        in_specs=specs,
        out_specs=out_specs or [IN_VMEM] * len(outs),
        scratch_shapes=list(scratch),
        input_output_aliases=aliases or {},
        compiler_params=pltpu.CompilerParams(vmem_limit_bytes=limit << 20),
    )(*operands)


def band_number(row_ref, offsets, k):
    if len(offsets) == 1:
        return row_ref[offsets[0]]
    return row_ref[offsets[0] + k * (offsets[1] - offsets[0])]


def stream(count, sources, weights, done, use):
    ways = len(sources)

    def copy(k, w):
        slot = k * ways + w
        return pltpu.make_async_copy(sources[w](k), weights.at[slot], done.at[slot])

    for k in range(count):
        for w in range(ways):
            copy(k, w).start()

    def step(k):
        for w in range(ways):
            copy(k, w).wait()
            use(k, w, weights.at[k * ways + w])

    if count == 1:
        return lambda: step(0)

    def run():
        def body(k, _):
            step(k)
            return 0

        lax.fori_loop(0, count, body, 0)

    return run


def rows_as_lanes(vectors):
    rows = vectors[0].shape[0]
    lane = lax.broadcasted_iota(jnp.int32, (rows, 128), 1)
    packed = jnp.zeros((rows, 128), f32)
    for k, vector in enumerate(vectors):
        packed = jnp.where(lane == k, vector, packed)
    return packed.T[:8]


def lanes_as_columns(vectors):
    rows = vectors[0].shape[1]
    line = lax.broadcasted_iota(jnp.int32, (128, rows), 0)
    packed = jnp.zeros((128, rows), f32)
    for k, vector in enumerate(vectors):
        packed = jnp.where(line == k, vector, packed)
    return packed.T


def split_terms(lanes):
    high = lanes.astype(bf16).astype(f32)
    rest = lanes - high
    middle = rest.astype(bf16).astype(f32)
    low = rest - middle
    top = jnp.concatenate([high, middle], axis=1)
    bottom = jnp.concatenate([low, jnp.zeros_like(low)], axis=1)
    return jnp.concatenate([top, bottom], axis=0).astype(bf16)


def joined_term(terms, k):
    half = terms.shape[1] // 2
    return terms[k : k + 1, :half] + terms[k : k + 1, half:] + terms[8 + k : 9 + k, :half]


def pieces_of(band):
    return band if isinstance(band, tuple) else (band,)


def pack_blocks(member, block, nodes):
    block_len, width = block.shape
    columns = width // nodes
    half = columns // 2

    def kernel(member_ref, block_ref, out):
        square = jnp.zeros((block_len, 1), f32)
        for d in range(nodes):
            part = block_ref[:, d * columns : (d + 1) * columns].astype(f32)
            square += jnp.sum(part * part, axis=1, keepdims=True)
        terms = split_terms(rows_as_lanes([lax.rsqrt(square / width + eps)]))
        for d in range(nodes):
            start = pl.multiple_of(d * columns + member_ref[0] * half, half)
            out[d, :block_len] = block_ref[:, pl.ds(start, half)]
            out[d, block_len:] = terms

    return call(
        kernel, [member, block], [IN_SMEM, IN_VMEM], [((nodes, block_len + AUX, half), bf16)]
    )[0]


def pick_blocks(ids, member, near, far):
    entries = ids.shape[0]
    block_len = near.shape[1] - AUX
    half = near.shape[2]

    def kernel(ids_ref, member_ref, near_ref, far_ref, band_out, inverse_out):
        first = member_ref[0] == 0
        for e in range(entries):
            mine, other = near_ref[ids_ref[e]], far_ref[ids_ref[e]]
            part = slice(e * block_len, (e + 1) * block_len)
            band_out[part, :half] = jnp.where(first, mine, other)[:block_len]
            band_out[part, half:] = jnp.where(first, other, mine)[:block_len]
            row = joined_term(mine[block_len:].astype(f32), 0)
            inverse_out[part] = lanes_as_columns([row])[:, 0:1]

    return call(
        kernel, [ids, member, near, far], [IN_SMEM, IN_SMEM, IN_VMEM, IN_VMEM],
        [((entries * block_len, 2 * half), bf16), ((entries * block_len, 1), f32)],
    )


def split_halves(back, ahead, middle):
    def kernel(back_ref, ahead_ref, first, second):
        first[...] = back_ref[:middle]
        second[...] = ahead_ref[middle:]

    columns = back.shape[1]
    return call(
        kernel, [back, ahead], [IN_VMEM] * 2,
        [((middle, columns), bf16), ((ahead.shape[0] - middle, columns), bf16)],
    )


def forward_bands(bands, row, offsets, gain_bands, inverse, gate_bands, up_bands, totals, final):
    bands = [pieces_of(band) for band in bands]
    flat = [piece for band in bands for piece in band]
    count = len(bands)
    rows, columns = inverse.shape[0], flat[0].shape[1]
    width = gate_bands.shape[2]
    last = final is not None
    far_offset = row.shape[0] // 2

    def kernel(row_ref, *refs):
        refs = list(refs)
        take = lambda k: [refs.pop(0) for _ in range(k)]
        band_refs = [take(len(band)) for band in bands]
        gain_ref, inverse_ref, gate_hbm, up_hbm = take(4)
        if totals:
            take(2)
        head_ref, down_hbm = take(2) if last else (None, None)
        totals_out = take(2)
        (scaled_out,) = take(1)
        if last:
            hidden_out, score_out, far_up, far_down = take(4)
        weights, done = take(2)

        def use(k, w, block):
            totals_out[w][...] += dot(scaled_out[k], block[...], 1, 0)

        run = stream(
            count,
            [
                lambda k: gate_hbm.at[band_number(row_ref, offsets, k)],
                lambda k: up_hbm.at[band_number(row_ref, offsets, k)],
            ],
            weights, done, use,
        )
        if last:
            far_weights, far_done = refs
            start = pl.multiple_of(row_ref[far_offset] * columns, columns)
            far_copy = pltpu.make_async_copy(
                down_hbm.at[:, pl.ds(start, columns)], far_weights, far_done
            )
            far_copy.start()
        for k in range(count):
            start = 0
            for ref in band_refs[k]:
                part = slice(start, start + ref.shape[0])
                scaled_out[k, part] = (
                    ref[...].astype(f32) * inverse_ref[part] * gain_ref[row_ref[offsets[k]]]
                ).astype(bf16)
                start += ref.shape[0]
        if not totals:
            for out in totals_out:
                out[...] = jnp.zeros_like(out)
        run()
        if last:
            gate_out, up_out = totals_out

            def finish(i, _):
                part = pl.ds(pl.multiple_of(i * STRIPE, STRIPE), STRIPE)
                share = jnp.zeros((STRIPE, CHUNK), f32)
                for c in range(0, width, CHUNK):
                    some = slice(c, c + CHUNK)
                    gate = gate_out[part, some]
                    hidden = (gate * jax.nn.sigmoid(gate) * up_out[part, some]).astype(bf16)
                    hidden_out[part, some] = hidden
                    share += hidden.astype(f32) * head_ref[:, some]
                score_out[part] = jnp.sum(share, axis=1, keepdims=True)
                return 0

            lax.fori_loop(0, rows // STRIPE, finish, 0)
            far_copy.wait()
            far = dot(hidden_out[...], far_weights[...], 1, 0).astype(bf16)
            far_up[...] = far[: rows // 2]
            far_down[...] = far[rows // 2 :]

    operands = [row] + flat + [gain_bands, inverse, gate_bands, up_bands]
    specs = [IN_SMEM] + [IN_VMEM] * (len(flat) + 2) + [IN_HBM, IN_HBM]
    aliases = {}
    if totals:
        aliases = {len(operands): 0, len(operands) + 1: 1}
        operands += list(totals)
        specs += [IN_VMEM] * 2
    outs = [((rows, width), f32)] * 2 + [((count, rows, columns), bf16)]
    scratch = [
        pltpu.VMEM((2 * count, columns, width), bf16), pltpu.SemaphoreType.DMA((2 * count,))
    ]
    if last:
        operands += list(final)
        specs += [IN_VMEM, IN_HBM]
        outs += [((rows, width), bf16), ((rows, 1), f32)] + [((rows // 2, columns), bf16)] * 2
        scratch += [pltpu.VMEM((width, columns), bf16), pltpu.SemaphoreType.DMA]
    out = call(kernel, operands, specs, outs, scratch, 8 + 4 * count, aliases)
    return out[:2], out[2], out[3:]


def pair_scales(notes, labels_ref, rows, entries, width):
    square, score = joined_term(notes, 0), joined_term(notes, 1)
    inverse_out = lax.rsqrt(square / width + eps)
    scores = inverse_out * score
    block_len = rows // entries
    rewards = [
        jnp.sum(scores[:, e * block_len : (e + 1) * block_len], axis=1, keepdims=True) / block_len
        for e in range(entries)
    ]
    drewards = [jnp.zeros((1, 1), f32) for _ in range(entries)]
    loss = jnp.zeros((1, 1), f32)
    for p in range(labels_ref.shape[0]):
        select = [
            (labels_ref[p, 0] == e).astype(f32) - (labels_ref[p, 1] == e).astype(f32)
            for e in range(entries)
        ]
        margin = sum(select[e] * rewards[e] for e in range(entries))
        loss += jnp.maximum(-margin, 0.0) + jnp.log1p(jnp.exp(-jnp.abs(margin)))
        weight = -jax.nn.sigmoid(-margin) * loss_scale
        drewards = [drewards[e] + select[e] * weight for e in range(entries)]
    lane = lax.broadcasted_iota(jnp.int32, (1, rows), 1)
    dscore = jnp.zeros((1, rows), f32)
    for e in range(entries):
        dscore = jnp.where(lane // block_len == e, drewards[e] / block_len, dscore)
    head_scale = inverse_out * dscore
    columns = lanes_as_columns([head_scale, inverse_out * head_scale * scores / width])
    return loss, columns[:, 0:1], columns[:, 1:2]


def backward_bands(bands, row, offsets, w_down, rows, total, final):
    bands = [pieces_of(band) for band in bands]
    flat = [piece for band in bands for piece in band]
    count = len(bands)
    columns = flat[0].shape[1]
    width, model_width = w_down.shape
    others = final[6] if final else []
    far_offset = row.shape[0] // 2

    def kernel(row_ref, *refs):
        refs = list(refs)
        take = lambda k: [refs.pop(0) for _ in range(k)]
        band_refs = [take(len(band)) for band in bands]
        (down_hbm,) = take(1)
        if total is not None:
            take(1)
        if final:
            gate_ref, up_ref, head_ref, labels_ref, gate_hbm, up_hbm = take(6)
            other_refs = take(len(others))
        (back_ref,) = take(1)
        if final:
            grads_out, inner_out, loss_out, head_scale, summed_scale, far_up, far_down = take(7)
        weights, done, kept = take(3)

        def use(k, w, block):
            back_ref[...] += dot(kept[k], block[...], 1, 1)

        def source(k):
            start = pl.multiple_of(band_number(row_ref, offsets, k) * columns, columns)
            return down_hbm.at[:, pl.ds(start, columns)]

        run = stream(count, [source], weights, done, use)
        if final:
            inner, far_weights, far_done = refs
            far_copies = [
                pltpu.make_async_copy(
                    source.at[row_ref[far_offset]], far_weights.at[w], far_done.at[w]
                )
                for w, source in enumerate((gate_hbm, up_hbm))
            ]
            for one in far_copies:
                one.start()
        for k in range(count):
            start = 0
            for ref in band_refs[k]:
                size = min(ref.shape[0], rows - start)
                kept[k, start : start + size] = ref[:size]
                start += size
        if total is None:
            back_ref[...] = jnp.zeros_like(back_ref)
        if final:
            tail = band_refs[-1][-1]
            notes = tail[tail.shape[0] - AUX :].astype(f32)
            for ref in other_refs:
                notes += ref[rows:].astype(f32)
            loss, head_column, summed_column = pair_scales(
                notes, labels_ref, rows, final[7], model_width
            )
            loss_out[...] = loss
            head_scale[...] = head_column
            summed_scale[...] = summed_column
        run()
        if not final:
            return

        def finish(i, _):
            part = pl.ds(pl.multiple_of(i * STRIPE, STRIPE), STRIPE)
            head_factor, summed_factor = head_scale[part], summed_scale[part]
            share = jnp.zeros((STRIPE, CHUNK), f32)
            for c in range(0, width, CHUNK):
                some = slice(c, c + CHUNK)
                gate, up = gate_ref[part, some], up_ref[part, some]
                sigmoid = jax.nn.sigmoid(gate)
                dhidden = head_factor * head_ref[:, some] - summed_factor * back_ref[part, some]
                dgate = (dhidden * up * sigmoid * (1.0 + gate * (1.0 - sigmoid))).astype(bf16)
                dup = (dhidden * (gate * sigmoid)).astype(bf16)
                grads_out[0, part, some] = dgate
                grads_out[1, part, some] = dup
                share += dgate.astype(f32) * gate + dup.astype(f32) * up
            inner[part] = jnp.sum(share, axis=1, keepdims=True)
            return 0

        lax.fori_loop(0, rows // STRIPE, finish, 0)
        lanes = rows_as_lanes([inner[...]])
        inner_out[...] = lanes
        far_copies[0].wait()
        far = dot(grads_out[0], far_weights[0], 1, 1)
        far_copies[1].wait()
        far += dot(grads_out[1], far_weights[1], 1, 1)
        middle = rows // 2
        far_up[:middle] = far[:middle].astype(bf16)
        far_down[...] = far[middle:].astype(bf16)
        pad = jnp.zeros((AUX - 8, columns), f32)
        far_up[middle:] = jnp.concatenate([high_low(lanes), pad], axis=0).astype(bf16)

    operands = [row] + flat + [w_down]
    specs = [IN_SMEM] + [IN_VMEM] * len(flat) + [IN_HBM]
    aliases = {}
    if total is not None:
        aliases = {len(operands): 0}
        operands.append(total)
        specs.append(IN_VMEM)
    scratch = [
        pltpu.VMEM((count, width, columns), bf16), pltpu.SemaphoreType.DMA((count,)),
        pltpu.VMEM((count, rows, columns), bf16),
    ]
    outs = [((rows, width), f32)]
    if final:
        operands += list(final[:6]) + list(others)
        specs += [IN_VMEM] * 3 + [IN_SMEM] + [IN_HBM] * 2 + [IN_VMEM] * len(others)
        outs += [
            ((2, rows, width), bf16), ((8, rows), f32), ((1, 1), f32), ((rows, 1), f32),
            ((rows, 1), f32), ((rows // 2 + AUX, columns), bf16), ((rows // 2, columns), bf16),
        ]
        scratch += [
            pltpu.VMEM((rows, 1), f32), pltpu.VMEM((2, columns, width), bf16),
            pltpu.SemaphoreType.DMA((2,)),
        ]
    return call(kernel, operands, specs, outs, scratch, 10 + 3 * count, aliases)


def out_parts(row, offsets, hidden, w_down, columns):
    count = len(offsets)
    rows, width = hidden.shape

    def kernel(row_ref, hidden_ref, down_hbm, out, weights, done):
        def use(k, w, block):
            out[k] = dot(hidden_ref[...], block[...], 1, 0)

        def source(k):
            start = pl.multiple_of(band_number(row_ref, offsets, k) * columns, columns)
            return down_hbm.at[:, pl.ds(start, columns)]

        stream(count, [source], weights, done, use)()

    return call(
        kernel, [row, hidden, w_down], [IN_SMEM, IN_VMEM, IN_HBM],
        [((count, rows, columns), f32)],
        [pltpu.VMEM((count, width, columns), bf16), pltpu.SemaphoreType.DMA((count,))],
        4 + 3 * count,
    )[0]


def scaled_parts(row, offsets, grads, gate_bands, up_bands, down):
    count = len(offsets)
    rows, width = grads.shape[1:]
    columns = gate_bands.shape[1]
    order, first, bands, hidden_t, head_bands, head_scale, summed_scale, before = down
    flat = [piece for band in bands for piece in pieces_of(band)]
    extra = len(bands)
    nodes = gate_bands.shape[0]

    def kernel(row_ref, order_ref, grads_ref, gate_hbm, up_hbm, hidden_ref, head_ref,
               head_scale_ref, summed_scale_ref, *refs):
        band_refs = list(refs[: len(flat)])
        out, down_hbm, weights, done, made, sent, kept = refs[-7:]

        def use(k, w, block):
            term = dot(grads_ref[w], block[...], 1, 1)
            if w:
                out[k] += term
            else:
                out[k] = term

        run = stream(
            count,
            [
                lambda k: gate_hbm.at[band_number(row_ref, offsets, k)],
                lambda k: up_hbm.at[band_number(row_ref, offsets, k)],
            ],
            weights, done, use,
        )
        for j, band in enumerate(bands):
            start = 0
            for _ in pieces_of(band):
                ref = band_refs.pop(0)
                size = min(ref.shape[0], rows - start)
                kept[j, start : start + size] = ref[:size]
                start += size

        def leave(j):
            start = pl.multiple_of(order_ref[first + j] * columns, columns)
            return pltpu.make_async_copy(
                made.at[j], down_hbm.at[:, pl.ds(start, columns)], sent.at[j]
            )

        def make(j, _):
            dsummed = (
                head_scale_ref[...] * head_ref[order_ref[first + j]]
                - summed_scale_ref[...] * kept[j].astype(f32)
            )
            made[j] = dot(hidden_ref[...], dsummed.astype(bf16), 1, 0).astype(bf16)
            leave(j).start()
            return 0

        lax.fori_loop(0, extra, make, 0)
        run()
        for j in range(extra):
            leave(j).wait()

    operands = [row, order, grads, gate_bands, up_bands, hidden_t, head_bands, head_scale]
    operands += [summed_scale] + flat
    specs = [IN_SMEM, IN_SMEM, IN_VMEM, IN_HBM, IN_HBM] + [IN_VMEM] * (4 + len(flat))
    aliases = None
    if before is not None:
        aliases = {len(operands): 1}
        operands.append(before)
        specs.append(IN_HBM)
    return call(
        kernel, operands, specs,
        [((count, rows, columns), f32), ((width, nodes * columns), bf16)],
        [
            pltpu.VMEM((2 * count, columns, width), bf16),
            pltpu.SemaphoreType.DMA((2 * count,)),
            pltpu.VMEM((extra, width, columns), bf16), pltpu.SemaphoreType.DMA((extra,)),
            pltpu.VMEM((extra, rows, columns), bf16),
        ],
        6 + 4 * count + 3 * extra, aliases, [IN_VMEM, IN_HBM],
    )


def high_low(row):
    high = row.astype(bf16).astype(f32)
    return jnp.concatenate([high, row - high], axis=1)


def add_arrival(parts, way, came, inner):
    rows, columns = parts.shape[1:]
    middle = rows // 2
    tail = 0 if inner is None else AUX
    size = min(came.shape[0] // middle * middle, rows)
    has_inner = came.shape[0] > size

    def kernel(parts_ref, came_ref, *refs):
        out = refs[-1]
        start = 0 if size == rows or way == 0 else middle
        part = slice(start, start + size)
        out[part] = (parts_ref[way, part] + came_ref[:size].astype(f32)).astype(bf16)
        if size < rows:
            rest = slice(middle - start, rows - start)
            out[rest] = parts_ref[way, rest].astype(bf16)
        if tail:
            row = refs[0][...]
            if has_inner:
                terms = came_ref[size:].astype(f32)[:8]
                row = row + terms[:, : columns // 2] + terms[:, columns // 2 :]
            pad = jnp.zeros((AUX - 8, columns), f32)
            out[rows:] = jnp.concatenate([high_low(row), pad], axis=0).astype(bf16)

    operands = [parts, came] + ([] if inner is None else [inner])
    return call(
        kernel, operands, [IN_VMEM] * len(operands), [((rows + tail, columns), bf16)]
    )[0]


def finish_summed(own, from_back, from_ahead, band, head_row, score):
    rows, columns = own.shape[1:]

    def kernel(own_ref, back_ref, ahead_ref, band_ref, head_ref, score_ref, summed_out, message):
        inputs = band_ref[...].astype(f32)
        summed = inputs + (
            own_ref[0] + (back_ref[...].astype(f32) + ahead_ref[...].astype(f32))
        )
        summed_out[...] = summed
        message[:rows] = summed.astype(bf16)
        square = jnp.sum(summed * summed, axis=1, keepdims=True)
        share = score_ref[...] + jnp.sum(inputs * head_ref[...], axis=1, keepdims=True)
        message[rows:] = split_terms(rows_as_lanes([square, share]))

    return call(
        kernel, [own, from_back, from_ahead, band, head_row, score], [IN_VMEM] * 6,
        [((rows, columns), f32), ((rows + AUX, columns), bf16)],
    )


def finish_rows(member, own, from_back, from_ahead, inner, band, summed, inverse, gain_row,
                head_row, head_scale, summed_scale, final_row, score_row, entries, width):
    rows, columns = own.shape[1:]
    block_len = rows // entries
    half = block_len // 2

    def kernel(member_ref, own_ref, back_ref, ahead_ref, inner_ref, band_ref, summed_ref,
               inverse_ref, gain_ref, head_ref, head_scale_ref, summed_scale_ref, final_ref,
               score_ref, kept_out, given_out, ffn_out, head_out, final_out, drows):
        dscaled = own_ref[0] + (back_ref[:rows].astype(f32) + ahead_ref[:rows].astype(f32))
        came = (back_ref[rows:].astype(f32) + ahead_ref[rows:].astype(f32))[:8]
        lanes = inner_ref[...] + came[:, : columns // 2] + came[:, columns // 2 :]
        inner_column = lanes_as_columns([lanes[0:1]])[:, 0:1]
        inverse_in = inverse_ref[...]
        normed = band_ref[...].astype(f32) * inverse_in
        ffn_out[...] = jnp.sum(dscaled * normed, axis=0, keepdims=True)
        summed = summed_ref[...]
        weighted = jnp.sum(head_scale_ref[...] * summed, axis=0, keepdims=True)
        head_out[...] = final_ref[...] * weighted
        final_out[...] = score_ref[...] * weighted
        dsummed = head_scale_ref[...] * head_ref[...] - summed_scale_ref[...] * summed
        drows[...] = (
            inverse_in * (dscaled * gain_ref[...] - normed * (inner_column / width)) + dsummed
        ).astype(bf16)
        for e in range(entries):
            for out, which in ((kept_out, member_ref[0]), (given_out, 1 - member_ref[0])):
                start = pl.multiple_of(e * block_len + which * half, half)
                out[e] = drows[pl.ds(start, half)]

    return call(
        kernel,
        [member, own, from_back, from_ahead, inner, band, summed, inverse, gain_row, head_row,
         head_scale, summed_scale, final_row, score_row],
        [IN_SMEM] + [IN_VMEM] * 13,
        [((entries, half, columns), bf16)] * 2 + [((1, columns), f32)] * 3,
        [pltpu.VMEM((rows, columns), bf16)],
    )


def route_rows(ids, other_ids, kept, taken, blocks):
    entries, half, columns = kept.shape

    def kernel(ids_ref, other_ref, kept_ref, taken_ref, out):
        def route(b, _):
            sums = []
            for listed, value in ((ids_ref, kept_ref), (other_ref, taken_ref)):
                total = sum(
                    jnp.where(listed[e] == b, value[e].astype(f32), 0.0) for e in range(entries)
                )
                sums.append(total.astype(bf16).astype(f32))
            out[b] = (sums[0] + sums[1]).astype(bf16)
            return 0

        lax.fori_loop(0, blocks, route, 0)

    return call(
        kernel, [ids, other_ids, kept, taken], [IN_SMEM, IN_SMEM, IN_VMEM, IN_VMEM],
        [((blocks, half, columns), bf16)],
    )[0]


def assemble_block(member, mine, other):
    nodes, half, columns = mine.shape

    def kernel(member_ref, mine_ref, other_ref, out):
        for value, which in ((mine_ref, member_ref[0]), (other_ref, 1 - member_ref[0])):
            part = pl.ds(pl.multiple_of(which * half, half), half)
            for d in range(nodes):
                out[part, d * columns : (d + 1) * columns] = value[d]

    return call(
        kernel, [member, mine, other], [IN_SMEM, IN_VMEM, IN_VMEM],
        [((2 * half, nodes * columns), bf16)],
    )[0]


def turned(value):
    def kernel(value_ref, out):
        out[...] = value_ref[...].T

    return call(kernel, [value], [IN_VMEM], [(value.shape[::-1], value.dtype)])[0]


def whole(*shape):
    zeros = (0,) * len(shape)
    return pl.BlockSpec(shape, lambda *_: zeros)


def grid_call(kernel, index, operands, specs, outs, out_specs, steps, scratch, aliases=None):
    return pl.pallas_call(
        kernel,
        out_shape=[jax.ShapeDtypeStruct(shape, dtype) for shape, dtype in outs],
        grid_spec=pltpu.PrefetchScalarGridSpec(
            num_scalar_prefetch=1, grid=(steps,), in_specs=specs, out_specs=out_specs,
            scratch_shapes=list(scratch),
        ),
        input_output_aliases=aliases or {},
        compiler_params=pltpu.CompilerParams(vmem_limit_bytes=20 << 20),
    )(index, *operands)


def weight_grads(index, stacks, grads):
    nodes = sum(stack.shape[0] for stack in stacks)
    _, rows, columns = stacks[0].shape
    width = grads.shape[2]

    def kernel(index_ref, *refs):
        grads_ref, gate_out, up_out, kept, done = refs[len(stacks) :]

        @pl.when(pl.program_id(0) == 0)
        def _():
            copies = []
            start = 0
            for n, ref in enumerate(refs[: len(stacks)]):
                copies.append(
                    pltpu.make_async_copy(
                        ref, kept.at[pl.ds(start, ref.shape[0])], done.at[n]
                    )
                )
                copies[-1].start()
                start += ref.shape[0]
            for one in copies:
                one.wait()

        scaled = kept[pl.program_id(0)].T
        gate_out[0] = dot(scaled, grads_ref[0], 1, 0).astype(bf16)
        up_out[0] = dot(scaled, grads_ref[1], 1, 0).astype(bf16)

    out = pl.BlockSpec((1, columns, width), lambda b, idx: (idx[b], 0, 0))
    stacks = [pltpu.with_memory_space_constraint(stack, pltpu.HBM) for stack in stacks]
    return grid_call(
        kernel, index, stacks + [grads], [IN_HBM] * len(stacks) + [IN_VMEM],
        [((nodes, columns, width), bf16)] * 2, [out, out], nodes,
        [
            pltpu.VMEM((nodes, rows, columns), bf16),
            pltpu.SemaphoreType.DMA((len(stacks),)),
        ],
    )


def after(values, *others):
    return lax.optimization_barrier(tuple(values) + tuple(others))[: len(values)]


def ring_body(features, blocks, pair_labels, ffn_gain, final_gain, score_head, w_gate, w_up, w_down):
    nodes = lax.axis_size("fsdp")
    position = lax.axis_index("fsdp")
    member = lax.axis_index("member").reshape(1)
    swap = [(0, 1), (1, 0)]
    ring = Ring(nodes, position)
    half = ring.half
    block_len, width = features.shape[1:]
    columns = width // nodes
    ids = blocks[0]
    entries = ids.shape[0]
    rows = entries * block_len
    middle = rows // 2
    w_gate = w_gate[0]
    w_up = w_up[0]
    w_down = w_down[0]
    hidden_count = w_gate.shape[1]
    gate_bands = w_gate.reshape(nodes, columns, hidden_count)
    up_bands = w_up.reshape(nodes, columns, hidden_count)
    gain_head = final_gain[0] * score_head[0]
    gain_bands = ffn_gain.reshape(nodes, 1, columns)
    head_bands = gain_head.reshape(nodes, 1, columns)

    def share(vector):
        return lax.dynamic_slice_in_dim(vector, position * columns, columns, 0)[None]

    other_ids = lax.ppermute(ids, "member", swap)
    sent = pack_blocks(member, features[0], nodes)
    near = lax.all_to_all(sent, "fsdp", split_axis=0, concat_axis=0, tiled=True)
    head_parts = jnp.stack(three_terms(gain_head))
    head_down = jnp.sum(contract(head_parts, w_down, 1, 1), axis=0)[None]
    visits = [0]
    for step in range(1, half):
        visits += [nodes - step, step]
    order = ring.visited(visits + [half], position)
    gain_row, head_row, final_row, score_row = (
        share(vector) for vector in (ffn_gain[0], gain_head, final_gain[0], score_head[0])
    )
    near, other_ids, ring.row, order, gain_row, head_row, final_row, score_row = after(
        [near, other_ids, ring.row, order, gain_row, head_row, final_row, score_row], head_down
    )
    far = lax.ppermute(near, "member", swap)
    band, inverse_in = pick_blocks(ids, member, near, far)

    def gather(own, visit, extra=None):
        back = ahead = own
        total = None
        pending, pending_offsets = [own], [0]
        order = []
        for step in range(1, half + 1):
            if step < half:
                back, ahead = ring.up(back), ring.down(ahead)
                arrived, offsets = [back, ahead], [nodes - step, step]
            else:
                first, second = split_halves(back, ahead, middle)
                arrived, offsets = [(ring.up(first), ring.down(second))], [step]
            total = visit(pending, pending_offsets, total)
            order += pending_offsets
            if step < half:
                done = list(total)
                if step == 1 and extra is not None:
                    done.append(extra)
                (back,), (ahead,) = after([back], *done), after([ahead], *done)
                arrived = [back, ahead]
            pending, pending_offsets = arrived, offsets
        order += pending_offsets
        return pending, pending_offsets, total, order

    scaled = []

    def forward(bands, offsets, total, final=None):
        total, new, rest = forward_bands(
            bands, ring.row, offsets, gain_bands, inverse_in, gate_bands, up_bands, total, final
        )
        scaled.append(new)
        return total if final is None else (total, rest)

    last, last_offsets, total, _ = gather(band, forward)
    (gate_pre, up_pre), (hidden, score, up_message, down_message) = forward(
        last, last_offsets, total, (head_down, w_down)
    )
    (held,) = after([hidden], up_message)
    back, ahead = ring.up(up_message), ring.down(down_message)
    for step in range(half - 1, 0, -1):
        parts = out_parts(ring.row, [step, nodes - step], held, w_down, columns)
        (held,) = after([held], back, ahead)
        back = ring.up(add_arrival(parts, 0, back, None))
        ahead = ring.down(add_arrival(parts, 1, ahead, None))
    own_part = out_parts(ring.row, [0], held, w_down, columns)
    summed_band, message = finish_summed(
        own_part, back, ahead, band, head_row, score
    )

    messages = []

    def backward(bands, offsets, total, final=None):
        messages.extend(bands)
        return backward_bands(
            bands, ring.row, offsets, w_down, rows, None if total is None else total[0], final
        )

    (held,) = after([hidden], message)
    hidden_t = turned(held)
    last, last_offsets, total, _ = gather(message, backward, hidden_t)
    _, grads, inner, loss, head_scale, summed_scale, up_message, down_message = backward(
        last, last_offsets, total,
        (
            gate_pre, up_pre, head_down, pair_labels[0], gate_bands, up_bands, list(messages),
            entries,
        ),
    )

    (held,) = after([grads], up_message)
    back, ahead = ring.up(up_message), ring.down(down_message)
    bounds = [0, 1, 3, 5, nodes]

    def parts_and_down(offsets, held, piece, before):
        start, stop = bounds[piece], bounds[piece + 1]
        return scaled_parts(
            ring.row, offsets, held, gate_bands, up_bands,
            (
                order, start, messages[start:stop], hidden_t, head_bands, head_scale,
                summed_scale, before,
            ),
        )

    grad_down = None
    for step in range(half - 1, 0, -1):
        parts, grad_down = parts_and_down(
            [step, nodes - step], held, half - 1 - step, grad_down
        )
        (held,) = after([held], back, ahead)
        back = ring.up(add_arrival(parts, 0, back, inner))
        ahead = ring.down(add_arrival(parts, 1, ahead, inner))
    own_part, grad_down = parts_and_down([0], held, half - 1, grad_down)
    kept, given, grad_ffn, grad_head, grad_final = finish_rows(
        member, own_part, back, ahead, inner, band, summed_band, inverse_in,
        gain_row, head_row, head_scale, summed_scale, final_row, score_row, entries, width,
    )

    (held,) = after([grads], given)
    taken = lax.ppermute(given, "member", swap)
    returned = route_rows(ids, other_ids, kept, taken, nodes)
    mine = lax.all_to_all(returned, "fsdp", split_axis=0, concat_axis=0, tiled=True)
    grad_gate, grad_up = weight_grads(order, scaled, held)
    (mine,) = after([mine], grad_gate, grad_up)
    other = lax.ppermute(mine, "member", swap)
    grad_features = assemble_block(member, mine, other)
    return (
        loss.reshape(1),
        grad_gate.reshape(1, width, hidden_count),
        grad_up.reshape(1, width, hidden_count),
        grad_down[None],
        grad_head,
        grad_final,
        grad_ffn,
        grad_features[None],
    )


def body(features, blocks, pair_labels, ffn_gain, final_gain, score_head, w_gate, w_up, w_down):
    nodes = lax.axis_size("fsdp")
    rows = blocks.shape[1] * features.shape[1]
    columns = features.shape[2] // nodes
    tiled = w_gate.shape[2] % 256 == 0 and columns == 2 * rows and rows % 256 == 0
    single = features.shape[0] == 1 and lax.axis_size("member") == 2
    chosen = ring_body if tiled and single and nodes == 8 else plain_body
    return chosen(
        features, blocks, pair_labels, ffn_gain, final_gain, score_head, w_gate, w_up, w_down
    )


def solution(mesh):
    in_specs = (
        P(("groups", "fsdp"), None, None),
        P(("groups", "member"), None),
        P(("groups", "member"), None, None),
        P("member", None),
        P("member", None),
        P("member", None),
        P("member", None, "fsdp"),
        P("member", None, "fsdp"),
        P("member", "fsdp", None),
    )
    out_specs = (
        P(("groups", "member")),
        P(("groups", "member"), None, "fsdp"),
        P(("groups", "member"), None, "fsdp"),
        P(("groups", "member"), "fsdp", None),
        P(("groups", "member"), "fsdp"),
        P(("groups", "member"), "fsdp"),
        P(("groups", "member"), "fsdp"),
        P(("groups", "fsdp"), None, None),
    )
    return jax.shard_map(body, mesh=mesh, in_specs=in_specs, out_specs=out_specs, check_vma=False)
```
